256 devices in a mesh: stream: 16 (over y, x), span: 16 (over z, core).
Axes of the slice: x: 4, y: 4, z: 8, core: 2. Of those that a mesh axis runs over, the one named last changes fastest.
Arguments:
- species: float32 [9, 128, 16, 2048], P(None, 'stream', None, 'span'), may hold values from -6 to 6
- history: float32 [16, 16, 32, 3, 9, 128], P('stream', 'span'), may hold values from -6 to 6
- flame_tiles: int32 [16, 16, 32], P('stream', 'span'), may hold values from 0 to 127, as said below
- owners: int32 [16, 16, 32, 1], P('stream', 'span'), may hold values from 0 to 15, as said below
- orders: int32 [16, 16, 32], P('stream', 'span'), may hold values from 1 to 3
- substeps: int32 [16, 16, 32], P('stream', 'span'), may hold values from 1 to 8
- levels: int32 [128, 16, 16], P('stream', None, 'span'), may hold values from 0 to 3
- mechanism: float32 [9, 9], replicated, may hold values from -2 to 2
Outputs:
- species_next: float32 [9, 128, 16, 2048], P(None, 'stream', None, 'span')
- chem_load: int32 [16, 16], P('stream', 'span')
The draws below stay inside these ranges and needn't reach their ends.
Inputs may be any that keep to these rules, and one draw needn't show every extreme that they name: `flame_tiles`: within one device's list the tile indices are distinct. `owners`: among the flame tiles of one device, no owner is named more than 6 times, and some owner exactly 6 times.
All inputs are finite; a program needn't handle non-finite values.
Results may differ from the reference program's by a relative error of at most 0.0003.
Values sent between devices are 32-bit elements; how exact they have to be, the bound alone decides.
A program may use at most 64 MiB of HBM per device.

```python
import jax
import jax.numpy as jnp
from jax import lax

NS = 9
CZ = 8
NX = 16
CY = 128
HORD = 3
SUBMAX = 8
TILES_DEV = 128
FLAME_DEV = 32
CAP = 6
SGROUPS = 16
SPANS = 16
NZ = 128
NY = 2048


def draw_flame_tiles(key, part):
    key_list = jax.random.split(jax.random.fold_in(key, 11), SGROUPS * SPANS)

    def selector(key_item):
        return jax.random.permutation(key_item, TILES_DEV)[:FLAME_DEV].astype(jnp.int32)
    return jax.vmap(selector)(key_list).reshape((SGROUPS, SPANS, FLAME_DEV))


def draw_owners(key, part):
    key_list = jax.random.split(jax.random.fold_in(key, 31), SGROUPS * SPANS)
    span_ids = jnp.arange(SPANS, dtype=jnp.int32)[None, :, None]
    slot_ids = jnp.arange(FLAME_DEV, dtype=jnp.int32)[None, None, :]
    others = (span_ids + 1 + (slot_ids - CAP) % (SPANS - 1)) % SPANS
    base = jnp.where(slot_ids < CAP, span_ids, others)
    base = jnp.broadcast_to(base, (SGROUPS, SPANS, FLAME_DEV)).reshape((SGROUPS * SPANS, FLAME_DEV))

    def shuffle(key_item, row_item):
        order_item = jax.random.permutation(key_item, FLAME_DEV)
        return row_item[order_item]
    mixed = jax.vmap(shuffle)(key_list, base)
    return mixed.reshape((SGROUPS, SPANS, FLAME_DEV, 1)).astype(jnp.int32)


def draw_substeps(key, part):
    base_key = jax.random.fold_in(key, 21)
    key_heavy, key_high, key_low = jax.random.split(base_key, 3)
    heavy_keys = jax.random.split(key_heavy, SGROUPS)

    def ranking(key_item):
        return jax.random.permutation(key_item, SPANS)
    heavy = jax.vmap(ranking)(heavy_keys) < 3
    high_steps = jax.random.randint(key_high, (SGROUPS, SPANS, FLAME_DEV), 6, SUBMAX + 1)
    low_steps = jax.random.randint(key_low, (SGROUPS, SPANS, FLAME_DEV), 1, 3)
    steps = jnp.where(heavy[..., None], high_steps, low_steps)
    first = jnp.where(heavy, SUBMAX, steps[..., 0])
    steps = steps.at[..., 0].set(first)
    return steps.astype(jnp.int32)


def plant(values, rng, smallest, high):
    extent = values.shape
    index_at = [jax.random.randint(jax.random.fold_in(rng, axis), (), 0, extent[axis]) for axis in range(len(extent))]
    values = values.at[tuple(index_at)].set(smallest)
    longest = extent.index(max(extent))
    index_at[longest] = (index_at[longest] + 1) % extent[longest]
    return values.at[tuple(index_at)].set(high)


def steps_of(rng, dims, cuts, low, largest):
    def one(dim, parts):
        heights = jax.random.uniform(jax.random.fold_in(jax.random.fold_in(rng, 6), dim), (parts,), jnp.float32, low / len(cuts), largest / len(cuts))
        return jnp.repeat(jnp.exp(heights), dims[dim] // parts).reshape((-1,) + (1,) * (len(dims) - dim - 1))

    factor_of = one(*cuts[0])
    for cut in cuts[1:]:
        factor_of = factor_of * one(*cut)
    return factor_of


def centred(stream_key, shape, scale, bound, cuts=(), kind=jnp.bfloat16):
    values = jax.random.normal(stream_key, shape, jnp.float32) * scale
    if len(cuts) > 0:
        values = steps_of(stream_key, shape, cuts, -0.22, 0.18) * values
    return jnp.clip(values, min=-bound, max=bound).astype(kind)


def setup_inputs(seed: int = 0) -> dict:
    key_of = jax.random.split(jax.random.key(seed), 9)
    return {
        "species": centred(key_of[0], (NS, NZ, NX, NY), 1.0, 6.0, ((1, 16), (3, 16)), jnp.float32),
        "history": centred(key_of[1], (SGROUPS, SPANS, FLAME_DEV, HORD, NS, CY), 1.0, 6.0, ((0, 16), (1, 16)), jnp.float32),
        "flame_tiles": draw_flame_tiles(jax.random.fold_in(key_of[8], 71), 0),
        "owners": draw_owners(jax.random.fold_in(key_of[8], 71), 0),
        "orders": plant(jax.random.randint(key_of[4], (SGROUPS, SPANS, FLAME_DEV), 1, 4), jax.random.fold_in(key_of[4], 1), 1, 3).astype(jnp.int32),
        "substeps": draw_substeps(jax.random.fold_in(key_of[8], 71), 0),
        "levels": plant(jax.random.randint(key_of[6], (NZ, NX, SPANS), 0, 4), jax.random.fold_in(key_of[6], 1), 0, 3).astype(jnp.int32),
        "mechanism": centred(key_of[7], (NS, NS), NS ** -0.5, 2.0, (), jnp.float32),
    }


def bdf_tables(order):
    level_ids = jnp.arange(1, 4, dtype=jnp.int32)
    selector = (order[:, None] == level_ids[None, :]).astype(jnp.float32)
    predictor_table = jnp.array([[1.0, 0.0, 0.0], [2.0, -1.0, 0.0], [3.0, -3.0, 1.0]], jnp.float32)
    corrector_table = jnp.array([[1.0, 0.0, 0.0], [4.0 / 3.0, -1.0 / 3.0, 0.0], [18.0 / 11.0, -9.0 / 11.0, 2.0 / 11.0]], jnp.float32)
    beta_table = jnp.array([1.0, 2.0 / 3.0, 6.0 / 11.0], jnp.float32)
    high = lax.Precision.HIGHEST
    return (jnp.dot(selector, predictor_table, precision=high), jnp.dot(selector, corrector_table, precision=high), jnp.dot(selector, beta_table, precision=high))


def integrate(history, order, substeps, mechanism):
    high = lax.Precision.HIGHEST
    predictor, corrector, beta = bdf_tables(order)
    initial = history[:, 0]
    for substep_index in range(SUBMAX):
        guess = jnp.einsum("km,kmsc->ksc", predictor, history, precision=high)
        force = jnp.tanh(jnp.einsum("st,ktc->ksc", mechanism, guess, precision=high))
        fresh = jnp.einsum("km,kmsc->ksc", corrector, history, precision=high) + 0.5 * beta[:, None, None] * force
        moved = jnp.stack([fresh, history[:, 0], history[:, 1]], axis=1)
        active = (substeps > substep_index)[:, None, None, None]
        history = jnp.where(active, moved, history)
    divisor = jnp.maximum(substeps.astype(jnp.float32), 1.0)
    return (history[:, 0] - initial) / divisor[:, None, None]


def gauss_table(length, width):
    position = jnp.arange(length, dtype=jnp.float32)
    offset = (position[:, None] - position[None, :]) / width
    kernel = jnp.exp(-0.5 * offset * offset)
    return kernel / jnp.sum(kernel, axis=1, keepdims=True)


def sensor_of(rates):
    power = jnp.mean(rates * rates, axis=0, keepdims=True)
    return power / (power + 1.0)


def reference(species, history, flame_tiles, owners, orders, substeps, levels, mechanism):
    groups, span_count, flame_count = flame_tiles.shape

    def per_group(pieces):
        group_history, group_orders, group_steps = pieces
        flat = group_history.reshape((span_count * flame_count, HORD, NS, CY))
        result = integrate(flat, group_orders.reshape(-1), group_steps.reshape(-1), mechanism)
        return result.reshape((span_count, flame_count, NS, CY))

    tile_rate = lax.map(per_group, (history, orders, substeps))
    base = jnp.zeros((groups, span_count, CZ * NX, NS, CY), jnp.float32)
    group_ids = jnp.arange(groups, dtype=jnp.int32)[:, None, None]
    span_ids = jnp.arange(span_count, dtype=jnp.int32)[None, :, None]
    base = base.at[group_ids, span_ids, flame_tiles.astype(jnp.int32)].set(tile_rate)
    rates = base.reshape((groups, span_count, CZ, NX, NS, CY)).transpose(4, 0, 2, 3, 1, 5).reshape((NS, NZ, NX, NY))
    rows = jnp.concatenate([rates, sensor_of(rates)], axis=0)
    table = gauss_table(NZ, 2.0 * CZ)
    filtered = jnp.einsum("zk,rkxy->rzxy", table, rows, precision=lax.Precision.HIGHEST)
    fine_rates = filtered[:NS]
    fine_sensor = filtered[NS]
    class_ids = jnp.arange(4, dtype=jnp.int32)
    peak_values = jnp.array([2.5, 5.0, 10.0, 20.0], jnp.float32)
    peak = jnp.sum(jnp.where(levels[..., None] == class_ids, peak_values, 0.0), axis=-1)
    peak = jnp.repeat(peak, CY, axis=2)
    thick = 1.0 + (peak - 1.0) * fine_sensor
    padded = jnp.pad(species, ((0, 0), (1, 1), (1, 1), (1, 1)))
    beside_all = padded[:, 2:, 1:-1, 1:-1] + padded[:, :-2, 1:-1, 1:-1]
    beside_all = beside_all + padded[:, 1:-1, 2:, 1:-1] + padded[:, 1:-1, :-2, 1:-1]
    beside_all = beside_all + padded[:, 1:-1, 1:-1, 2:] + padded[:, 1:-1, 1:-1, :-2]
    spread = beside_all - 6.0 * species
    species_next = species + 0.02 * thick * spread + 4.0 * fine_rates / thick
    owner_ids = jnp.arange(span_count, dtype=jnp.int32)
    owned = (owners[..., 0][..., None] == owner_ids).astype(jnp.int32)
    chem_load = jnp.sum(owned * substeps[..., None], axis=(1, 2)).astype(jnp.int32)
    return species_next, chem_load
```

```python
import functools

import jax
import jax.numpy as jnp
from jax import lax
from jax.experimental import pallas as pl
from jax.experimental.pallas import tpu as pltpu
from jax.sharding import PartitionSpec as P

MESH = pl.DeviceIdType.MESH
F32 = jnp.float32
SUBMAX = 8
NS = 9
SIDE = 4
GROUPS = SIDE * SIDE
CHUNKS = 4
CHUNK_ORDER = (0, 2, 1, 3)


def iota(shape, dim):
    return lax.broadcasted_iota(jnp.int32, shape, dim)


def by_order(order, one, two, three):
    return jnp.where(order == 1, F32(one), jnp.where(order == 2, F32(two), F32(three)))


def column(row, size):
    wide = jnp.broadcast_to(row.astype(F32), (size, size))
    eye = iota((size, size), 0) == iota((size, size), 1)
    return jnp.sum(jnp.where(eye, wide, 0.0), axis=1, keepdims=True)


def kernel(
    spans,
    mech,
    species_hbm,
    history_hbm,
    tiles,
    owners,
    orders,
    steps,
    levels,
    out_hbm,
    load,
    hist,
    sp,
    outv,
    rate,
    sens,
    meta,
    share,
    coef,
    zh,
    yh,
    pack,
    spread,
    wts,
    hist_sem,
    sp_sem,
    out_sem,
    send_sem,
    recv_sem,
    small_send,
    small_recv,
    halo_send,
    halo_recv,
):
    me = lax.axis_index("stream")
    mp = lax.axis_index("span")
    sy, sx = me // SIDE, me % SIDE

    def at(dy, dx):
        return ((sy + dy + SIDE) % SIDE) * SIDE + (sx + dx + SIDE) % SIDE

    barrier = pltpu.get_barrier_semaphore()
    for d in range(1, GROUPS):
        pl.semaphore_signal(barrier, inc=1, device_id={"stream": (me + d) % GROUPS}, device_id_type=MESH)
    for d in range(1, spans):
        pl.semaphore_signal(barrier, inc=1, device_id={"span": (mp + d) % spans}, device_id_type=MESH)

    hist_copy = pltpu.make_async_copy(history_hbm, hist, hist_sem)
    hist_copy.start()
    sp_copy = pltpu.make_async_copy(species_hbm, sp, sp_sem)
    sp_copy.start()

    lane8 = iota((8, 128), 1)
    row8 = iota((8, 128), 0)
    order = jnp.broadcast_to(column(orders[...], 32), (32, 128))
    count = column(steps[...], 32)
    tile = column(tiles[...], 32)
    owner = column(owners[...], 32)
    coef[0] = by_order(order, 1.0, 2.0, 3.0)
    coef[1] = by_order(order, 0.0, -1.0, -3.0)
    coef[2] = by_order(order, 0.0, 0.0, 1.0)
    coef[3] = by_order(order, 1.0, 4.0 / 3.0, 18.0 / 11.0)
    coef[4] = by_order(order, 0.0, -1.0 / 3.0, -9.0 / 11.0)
    coef[5] = by_order(order, 0.0, 0.0, 2.0 / 11.0)
    coef[6] = by_order(order, 0.5, 0.5 * 2.0 / 3.0, 0.5 * 6.0 / 11.0)
    count_b = jnp.broadcast_to(count, (32, 128))
    coef[7] = count_b
    coef[8] = 1.0 / jnp.maximum(count_b, 1.0)

    tile_z = jnp.floor(tile * (1.0 / 16.0))
    tile_x = jnp.broadcast_to(tile - 16.0 * tile_z, (32, 128))
    tile_z = jnp.broadcast_to(tile_z + 8.0 * me.astype(F32), (32, 128))
    mine = (lane8 // 8 == me) & (lane8 % 8 == row8)
    table = jnp.zeros((8, 128), F32)
    for c in range(CHUNKS):
        for k, values in ((0, tile_z), (4, tile_x)):
            line = jnp.sum(jnp.where(mine, values[8 * c : 8 * c + 8], 0.0), axis=0, keepdims=True)
            table = jnp.where(row8 == c + k, jnp.broadcast_to(line, (8, 128)), table)
    meta[me] = table
    lane32 = iota((32, 128), 1).astype(F32)
    owed = jnp.sum(jnp.where(owner == lane32, count_b, 0.0), axis=0, keepdims=True)
    share[mp] = owed

    def send_chunk(c, src, dst):
        pltpu.make_async_remote_copy(
            src_ref=rate.at[c, src],
            dst_ref=rate.at[c, src],
            send_sem=send_sem,
            recv_sem=recv_sem.at[c, src],
            device_id={"stream": dst},
            device_id_type=MESH,
        ).start()

    def directions(c):
        return c < 2, 1 if c % 2 == 0 else -1

    def step_to(c, first, second):
        x_first, _ = directions(c)
        return at(second, first) if x_first else at(first, second)

    def forward(c, src, df, dg):
        _, e = directions(c)
        if dg == 0:
            if df == 0:
                send_chunk(c, src, step_to(c, e, 0))
                send_chunk(c, src, step_to(c, -e, 0))
            elif df == e:
                send_chunk(c, src, step_to(c, e, 0))
            send_chunk(c, src, step_to(c, 0, e))
            send_chunk(c, src, step_to(c, 0, -e))
        elif dg == e:
            send_chunk(c, src, step_to(c, 0, e))

    def arrive(c, df, dg):
        src = step_to(c, -df, -dg)
        pltpu.make_async_copy(rate.at[c, src], rate.at[c, src], recv_sem.at[c, src]).wait()
        forward(c, src, df, dg)

    hist_copy.wait()

    def chemistry(c):
        rows = slice(8 * c, 8 * c + 8)
        p1, p2, p3, a1, a2, a3, hb, cnt, inv = [coef[k, rows, :] for k in range(9)]
        h1, h2, h3 = [tuple(hist[m, s, rows, :] for s in range(NS)) for m in range(3)]

        def substep(n, carry):
            h1, h2, h3, last = carry
            guess = [p1 * h1[s] + p2 * h2[s] + p3 * h3[s] for s in range(NS)]
            active = cnt > n.astype(F32)
            fresh = []
            done = []
            for s in range(NS):
                total = mech[s, 0] * guess[0]
                for t in range(1, NS):
                    total = total + mech[s, t] * guess[t]
                y = a1 * h1[s] + a2 * h2[s] + a3 * h3[s] + hb * jnp.tanh(total)
                fresh.append(y)
                done.append(jnp.where(active, y, last[s]))
            return tuple(fresh), h1, h2, tuple(done)

        _, _, _, last = lax.fori_loop(0, SUBMAX, substep, (h1, h2, h3, h1))
        for s in range(NS):
            rate[c, me, s] = (last[s] - hist[0, s, rows, :]) * inv

    chemistry(CHUNK_ORDER[0])
    pl.semaphore_wait(barrier, (GROUPS - 1) + (spans - 1))
    forward(CHUNK_ORDER[0], me, 0, 0)
    for d in range(1, GROUPS):
        pltpu.make_async_remote_copy(
            meta.at[me], meta.at[me], small_send.at[0], small_recv.at[0], device_id={"stream": (me + d) % GROUPS}, device_id_type=MESH
        ).start()
    for d in range(1, spans):
        pltpu.make_async_remote_copy(
            share.at[mp], share.at[mp], small_send.at[1], small_recv.at[1], device_id={"span": (mp + d) % spans}, device_id_type=MESH
        ).start()
    for c in CHUNK_ORDER[1:]:
        chemistry(c)
        forward(c, me, 0, 0)

    sp_copy.wait()
    halo = [
        pltpu.make_async_remote_copy(
            sp.at[:, 7], zh.at[0], halo_send.at[0], halo_recv.at[0], device_id={"stream": (me + 1) % GROUPS}, device_id_type=MESH
        ),
        pltpu.make_async_remote_copy(
            sp.at[:, 0], zh.at[1], halo_send.at[1], halo_recv.at[1], device_id={"stream": (me + GROUPS - 1) % GROUPS}, device_id_type=MESH
        ),
    ]
    for copy in halo:
        copy.start()
    lane = iota((8, 16, 128), 2)
    packed = jnp.zeros((8, 16, 128), F32)
    for s in range(NS):
        turned = pltpu.roll(sp[s], 2 * s + 2, 2)
        packed = jnp.where((lane == 2 * s + 1) | (lane == 2 * s + 2), turned, packed)
    pack[...] = packed
    for k, dst in ((2, (mp + 1) % spans), (3, (mp + spans - 1) % spans)):
        copy = pltpu.make_async_remote_copy(
            pack, yh.at[k - 2], halo_send.at[k], halo_recv.at[k], device_id={"span": dst}, device_id_type=MESH
        )
        copy.start()
        halo.append(copy)

    def level(n):
        for c in CHUNK_ORDER:
            _, e = directions(c)
            hops = {0: 0, e: 1, -e: 1, 2 * e: 2}
            for df in hops:
                for dg in hops:
                    if hops[df] + hops[dg] == n:
                        arrive(c, df, dg)

    level(1)

    for copy in halo:
        copy.wait()
    below = jnp.where(me > 0, 1.0, 0.0).astype(F32)
    above = jnp.where(me < GROUPS - 1, 1.0, 0.0).astype(F32)
    left = jnp.where(mp > 0, 1.0, 0.0).astype(F32)
    right = jnp.where(mp < spans - 1, 1.0, 0.0).astype(F32)
    xs = iota((8, 16, 128), 1)
    edge = jnp.where(lane % 2 == 0, pltpu.roll(yh[1], 126, 2) * right, yh[0] * left)
    for s in range(NS):
        cells = sp[s]
        ends = pltpu.roll(edge, 127 - 2 * s, 2)
        zdown = jnp.concatenate([(zh[0, s] * below)[None], cells[:-1]], axis=0)
        zup = jnp.concatenate([cells[1:], (zh[1, s] * above)[None]], axis=0)
        xdown = jnp.where(xs == 0, 0.0, pltpu.roll(cells, 1, 1))
        xup = jnp.where(xs == 15, 0.0, pltpu.roll(cells, 15, 1))
        ydown = jnp.where(lane == 0, ends, pltpu.roll(cells, 1, 2))
        yup = jnp.where(lane == 127, ends, pltpu.roll(cells, 127, 2))
        spread[s] = zup + zdown + xup + xdown + yup + ydown - 6.0 * cells

    level(2)

    pltpu.make_async_copy(share.at[pl.ds(0, spans - 1)], share.at[pl.ds(0, spans - 1)], small_recv.at[1]).wait()
    owed = share[0]
    for g in range(1, spans):
        owed = owed + share[g]
    here = jnp.where(iota((1, 128), 1) == mp, owed, 0.0)
    load[...] = jnp.sum(here, axis=1, keepdims=True).astype(jnp.int32)

    pltpu.make_async_copy(meta.at[pl.ds(0, GROUPS - 1)], meta.at[pl.ds(0, GROUPS - 1)], small_recv.at[0]).wait()
    table = meta[0]
    for g in range(1, GROUPS):
        table = table + meta[g]
    cell = iota((128, 128), 0)
    cell_z = (8 * me + cell // 16).astype(F32)
    cell_x = (cell % 16).astype(F32)

    def gauss(other):
        offset = (cell_z - other) * (1.0 / 16.0)
        return jnp.exp(-0.5 * offset * offset)

    norm = 1.0 / jnp.sum(gauss(iota((128, 128), 1).astype(F32)), axis=1, keepdims=True)
    for c in range(CHUNKS):
        wts[c] = jnp.where(cell_x == table[c + 4 : c + 5], gauss(table[c : c + 1]) * norm, 0.0)

    level(3)
    level(4)

    for c in range(CHUNKS):
        power = jnp.zeros((GROUPS, 8, 128), F32)
        for s in range(NS):
            power = power + rate[c, :, s] * rate[c, :, s]
        power = power * (1.0 / NS)
        sens[c] = power / (power + 1.0)

    def filtered(parts):
        total = jnp.zeros((128, 128), F32)
        for c in range(CHUNKS):
            total = total + jnp.dot(
                wts[c], parts(c).reshape(128, 128), precision=lax.Precision.HIGHEST, preferred_element_type=F32
            )
        return total

    peaks = []
    for z in range(8):
        wide = jnp.broadcast_to(levels[z], (16, 16))
        eye = iota((16, 16), 0) == iota((16, 16), 1)
        kind = jnp.sum(jnp.where(eye, wide.astype(F32), 0.0), axis=1, keepdims=True)
        peaks.append(jnp.where(kind == 0, 1.5, jnp.where(kind == 1, 4.0, jnp.where(kind == 2, 9.0, 19.0))))
    peak = jnp.concatenate(peaks, axis=0).astype(F32)
    thick = 1.0 + peak * filtered(lambda c: sens[c])
    stretch = 0.02 * thick
    damp = 4.0 / thick
    outs = []
    for s in range(NS):
        fine = filtered(lambda c: rate[c, :, s])
        value = sp[s].reshape(128, 128) + stretch * spread[s].reshape(128, 128) + fine * damp
        outv[s] = value.reshape(8, 16, 128)
        copy = pltpu.make_async_copy(outv.at[s], out_hbm.at[s], out_sem.at[s])
        copy.start()
        outs.append(copy)
    for copy in outs:
        copy.wait()
    for c in range(CHUNKS):
        sent = rate.at[c, pl.ds(0, GROUPS - 1)]
        pltpu.make_async_copy(sent, sent, send_sem).wait()
    pltpu.make_async_copy(meta.at[pl.ds(0, GROUPS - 1)], meta.at[pl.ds(0, GROUPS - 1)], small_send.at[0]).wait()
    pltpu.make_async_copy(share.at[pl.ds(0, spans - 1)], share.at[pl.ds(0, spans - 1)], small_send.at[1]).wait()


def shards(spans, species, history, flame_tiles, owners, orders, substeps, levels, mechanism):
    states = jnp.transpose(history, (0, 1, 3, 4, 2, 5)).reshape(3, NS, 32, 128)
    vmem = pl.BlockSpec(memory_space=pltpu.VMEM)
    anywhere = pl.BlockSpec(memory_space=pl.ANY)
    out, load = pl.pallas_call(
        functools.partial(kernel, spans),
        out_shape=(
            jax.ShapeDtypeStruct(species.shape, F32),
            jax.ShapeDtypeStruct((1, 1), jnp.int32),
        ),
        in_specs=[pl.BlockSpec(memory_space=pltpu.SMEM), anywhere, anywhere] + [vmem] * 5,
        out_specs=(anywhere, vmem),
        scratch_shapes=[
            pltpu.VMEM((3, NS, 32, 128), F32),
            pltpu.VMEM((NS, 8, 16, 128), F32),
            pltpu.VMEM((NS, 8, 16, 128), F32),
            pltpu.VMEM((CHUNKS, GROUPS, NS, 8, 128), F32),
            pltpu.VMEM((CHUNKS, GROUPS, 8, 128), F32),
            pltpu.VMEM((GROUPS, 8, 128), F32),
            pltpu.VMEM((spans, 1, 128), F32),
            pltpu.VMEM((9, 32, 128), F32),
            pltpu.VMEM((2, NS, 16, 128), F32),
            pltpu.VMEM((2, 8, 16, 128), F32),
            pltpu.VMEM((8, 16, 128), F32),
            pltpu.VMEM((NS, 8, 16, 128), F32),
            pltpu.VMEM((CHUNKS, 128, 128), F32),
            pltpu.SemaphoreType.DMA,
            pltpu.SemaphoreType.DMA,
            pltpu.SemaphoreType.DMA((NS,)),
            pltpu.SemaphoreType.DMA,
            pltpu.SemaphoreType.DMA((CHUNKS, GROUPS)),
            pltpu.SemaphoreType.DMA((2,)),
            pltpu.SemaphoreType.DMA((2,)),
            pltpu.SemaphoreType.DMA((4,)),
            pltpu.SemaphoreType.DMA((4,)),
        ],
        compiler_params=pltpu.CompilerParams(collective_id=0, has_side_effects=True),
    )(
        mechanism,
        species,
        states,
        flame_tiles.reshape(1, 32),
        owners.reshape(1, 32),
        orders.reshape(1, 32),
        substeps.reshape(1, 32),
        jnp.transpose(levels, (0, 2, 1)),
    )
    return out, load


def solution(mesh):
    in_specs = (
        P(None, "stream", None, "span"),
        P("stream", "span", None, None, None, None),
        P("stream", "span", None),
        P("stream", "span", None, None),
        P("stream", "span", None),
        P("stream", "span", None),
        P("stream", None, "span"),
        P(),
    )
    out_specs = (P(None, "stream", None, "span"), P("stream", "span"))
    return jax.shard_map(
        functools.partial(shards, mesh.shape["span"]),
        mesh=mesh,
        in_specs=in_specs,
        out_specs=out_specs,
        check_vma=False,
    )
```

```python
import functools

import jax
import jax.numpy as jnp
from jax import lax
from jax.experimental import pallas as pl
from jax.experimental.pallas import tpu as pltpu
from jax.sharding import PartitionSpec as P

MESH = pl.DeviceIdType.MESH
F32 = jnp.float32
BF16 = jnp.bfloat16
SUBMAX = 8
NS = 9
SIDE = 4
GROUPS = SIDE * SIDE
CHUNKS = 4
ROWS = 8 * NS + 1
ORDER = (0, 2, 1, 3)


def iota(shape, dim):
    return lax.broadcasted_iota(jnp.int32, shape, dim)


def by_order(order, one, two, three):
    return jnp.where(order == 1, F32(one), jnp.where(order == 2, F32(two), F32(three)))


def column(row, size):
    wide = jnp.broadcast_to(row.astype(F32), (size, size))
    eye = iota((size, size), 0) == iota((size, size), 1)
    return jnp.sum(jnp.where(eye, wide, 0.0), axis=1, keepdims=True)


def sign(c):
    return 1 if c % 2 == 0 else -1


def arrivals():
    found = []
    for n in range(5):
        for c in ORDER:
            e = sign(c)
            hops = {0: 0, e: 1, -e: 1, 2 * e: 2}
            found += [(c, df, dg) for df in hops for dg in hops if hops[df] + hops[dg] == n]
    return found


def kernel(
    spans,
    mech,
    species_hbm,
    history_hbm,
    tiles,
    owners,
    orders,
    steps,
    levels,
    out,
    load_out,
    load,
    hist,
    sp,
    rate,
    share,
    coef,
    zh,
    yh,
    pack,
    spread,
    acc,
    hist_sem,
    sp_sem,
    send_sem,
    recv_sem,
    share_send,
    share_recv,
    halo_send,
    halo_recv,
):
    me = lax.axis_index("stream")
    mp = lax.axis_index("span")
    sy, sx = me // SIDE, me % SIDE

    hist_copy = pltpu.make_async_copy(history_hbm, hist, hist_sem)
    hist_copy.start()
    sp_copy = pltpu.make_async_copy(species_hbm, sp, sp_sem)
    sp_copy.start()

    def at(dy, dx):
        return ((sy + dy + SIDE) % SIDE) * SIDE + (sx + dx + SIDE) % SIDE

    after, before = (me + 1) % GROUPS, (me + GROUPS - 1) % GROUPS
    barrier = pltpu.get_barrier_semaphore()
    for peer in (at(0, 1), at(0, -1), at(1, 0), at(-1, 0), after, before):
        pl.semaphore_signal(barrier, inc=1, device_id={"stream": peer}, device_id_type=MESH)
    for d in range(1, spans):

        @pl.when(mp + d < spans)
        def _():
            pl.semaphore_signal(barrier, inc=1, device_id={"span": mp + d}, device_id_type=MESH)

    order = jnp.broadcast_to(column(orders[...], 32), (32, 128))
    count = column(steps[...], 32)
    tile = column(tiles[...], 32)
    owner = column(owners[...], 32)
    coef[0] = by_order(order, 1.0, 2.0, 3.0)
    coef[1] = by_order(order, 0.0, -1.0, -3.0)
    coef[2] = by_order(order, 0.0, 0.0, 1.0)
    coef[3] = by_order(order, 1.0, 4.0 / 3.0, 18.0 / 11.0)
    coef[4] = by_order(order, 0.0, -1.0 / 3.0, -9.0 / 11.0)
    coef[5] = by_order(order, 0.0, 0.0, 2.0 / 11.0)
    coef[6] = by_order(order, 0.5, 0.5 * 2.0 / 3.0, 0.5 * 6.0 / 11.0)
    count_b = jnp.broadcast_to(count, (32, 128))
    coef[7] = count_b
    coef[8] = 1.0 / jnp.maximum(count_b, 1.0)

    cell_of = jnp.broadcast_to(tile + (128 * me).astype(F32), (32, 128))
    mine = iota((8, 128), 1) % 8 == iota((8, 128), 0)
    for c in range(CHUNKS):
        rate[c, me, 8 * NS : ROWS, :] = jnp.sum(jnp.where(mine, cell_of[8 * c : 8 * c + 8], 0.0), axis=0, keepdims=True)
    lane32 = iota((32, 128), 1).astype(F32)
    share[mp] = jnp.sum(jnp.where(owner == lane32, count_b, 0.0), axis=0, keepdims=True)

    def send_chunk(c, src, dst):
        pltpu.make_async_remote_copy(
            src_ref=rate.at[c, src],
            dst_ref=rate.at[c, src],
            send_sem=send_sem,
            recv_sem=recv_sem.at[c, src],
            device_id={"stream": dst},
            device_id_type=MESH,
        ).start()

    def step_to(c, first, second):
        return at(second, first) if c < 2 else at(first, second)

    def forward(c, df, dg):
        src = step_to(c, -df, -dg)
        e = sign(c)
        if dg == 0:
            if df == 0:
                send_chunk(c, src, step_to(c, e, 0))
                send_chunk(c, src, step_to(c, -e, 0))
            elif df == e:
                send_chunk(c, src, step_to(c, e, 0))
            send_chunk(c, src, step_to(c, 0, e))
            send_chunk(c, src, step_to(c, 0, -e))
        elif dg == e:
            send_chunk(c, src, step_to(c, 0, e))

    def arrive(c, df, dg):
        if (df, dg) != (0, 0):
            src = step_to(c, -df, -dg)
            pltpu.make_async_copy(rate.at[c, src], rate.at[c, src], recv_sem.at[c, src]).wait()
            forward(c, df, dg)

    def chemistry(c):
        rows = slice(8 * c, 8 * c + 8)
        p1, p2, p3, a1, a2, a3, hb, cnt, inv = [coef[k, rows, :] for k in range(9)]
        h1, h2, h3 = [tuple(hist[m, s, rows, :] for s in range(NS)) for m in range(3)]

        def substep(n, carry):
            h1, h2, h3, last = carry
            guess = [p1 * h1[s] + p2 * h2[s] + p3 * h3[s] for s in range(NS)]
            active = cnt > n.astype(F32)
            fresh = []
            done = []
            for s in range(NS):
                total = mech[s, 0] * guess[0]
                for t in range(1, NS):
                    total = total + mech[s, t] * guess[t]
                y = a1 * h1[s] + a2 * h2[s] + a3 * h3[s] + hb * jnp.tanh(total)
                fresh.append(y)
                done.append(jnp.where(active, y, last[s]))
            return tuple(fresh), h1, h2, tuple(done)

        _, _, _, last = lax.fori_loop(0, SUBMAX, substep, (h1, h2, h3, h1))
        for s in range(NS):
            rate[c, me, 8 * s : 8 * s + 8, :] = (last[s] - hist[0, s, rows, :]) * inv

    hist_copy.wait()
    chemistry(ORDER[0])
    sp_copy.wait()
    lane = iota((8, 16, 128), 2)
    packed = jnp.zeros((8, 16, 128), F32)
    for s in range(NS):
        turned = pltpu.roll(sp[s], 2 * s + 2, 2)
        packed = jnp.where((lane == 2 * s + 1) | (lane == 2 * s + 2), turned, packed)
    pack[...] = packed
    chemistry(ORDER[1])
    chemistry(ORDER[2])
    pl.semaphore_wait(barrier, 6 + mp)
    for c in ORDER[:3]:
        forward(c, 0, 0)
    chemistry(ORDER[3])
    forward(ORDER[3], 0, 0)

    z_halo = [
        pltpu.make_async_remote_copy(
            sp.at[:, 7], zh.at[0], halo_send.at[0], halo_recv.at[0], device_id={"stream": after}, device_id_type=MESH
        ),
        pltpu.make_async_remote_copy(
            sp.at[:, 0], zh.at[1], halo_send.at[1], halo_recv.at[1], device_id={"stream": before}, device_id_type=MESH
        ),
    ]
    for copy in z_halo:
        copy.start()

    def send_share(dst):
        pltpu.make_async_remote_copy(
            share.at[mp], share.at[mp], share_send.at[dst], share_recv.at[mp], device_id={"span": dst}, device_id_type=MESH
        ).start()

    def wait_share(sem, k):
        pltpu.make_async_copy(share.at[k], share.at[k], sem.at[k]).wait()

    def halo_copy(slot, dst):
        return pltpu.make_async_remote_copy(
            pack, yh.at[slot], halo_send.at[2 + slot], halo_recv.at[2 + slot], device_id={"span": dst}, device_id_type=MESH
        )

    def wait_halo(sem, slot):
        pltpu.make_async_copy(yh.at[slot], yh.at[slot], sem.at[2 + slot]).wait()

    @pl.when(mp > 0)
    def _():
        halo_copy(1, mp - 1).start()

    for d in range(1, spans):

        @pl.when(mp >= d)
        def _():
            send_share(mp - d)

    cell = iota((128, 128), 0) + 128 * me
    cell_z = (cell // 16).astype(F32)
    cell_x = (cell % 16).astype(F32)
    lane2 = iota((1, 128), 1)

    def gauss(other):
        offset = (cell_z - other) * (1.0 / 16.0)
        return jnp.exp(-0.5 * offset * offset)

    norm = 1.0 / jnp.sum(gauss(iota((128, 128), 1).astype(F32)), axis=1, keepdims=True)

    def filter_part(slots, initial):
        refs = [(c, step_to(c, -df, -dg)) for c, df, dg in slots]
        cells = jnp.zeros((1, 128), F32)
        for k, (c, src) in enumerate(refs):
            cells = jnp.where(lane2 // 8 == k, rate[c, src, 8 * NS : ROWS, :], cells)
        z = jnp.floor(cells * (1.0 / 16.0))
        x = cells - 16.0 * z
        weight = jnp.where(cell_x == x, gauss(z) * norm, 0.0)
        high = weight.astype(BF16)
        low = (weight - high.astype(F32)).astype(BF16)
        left = jnp.concatenate([high, high, low], axis=1)

        def split(values):
            high = values.astype(BF16)
            low = (values - high.astype(F32)).astype(BF16)
            return jnp.concatenate([high, low, high], axis=0)

        values = [jnp.concatenate([rate[c, src, 8 * s : 8 * s + 8, :] for c, src in refs], axis=0) for s in range(NS)]
        power = values[0] * values[0]
        for s in range(1, NS):
            power = power + values[s] * values[s]
        power = power * (1.0 / NS)
        values = [power / (power + 1.0)] + values
        for k in range(5):
            right = jnp.concatenate([split(values[2 * k]), split(values[2 * k + 1])], axis=1)
            part = jnp.dot(left, right, preferred_element_type=F32)
            if not initial:
                part = part + acc[k]
            acc[k] = part

    events = arrivals()
    for event in events[:16]:
        arrive(*event)
    filter_part(events[:16], True)
    for event in events[16:32]:
        arrive(*event)
    filter_part(events[16:32], False)

    @pl.when(mp < spans - 1)
    def _():
        wait_halo(halo_recv, 1)
        halo_copy(0, mp + 1).start()

    for d in range(1, spans):

        @pl.when(mp + d < spans)
        def _():
            wait_share(share_recv, mp + d)
            send_share(mp + d)

    for event in events[32:48]:
        arrive(*event)
    filter_part(events[32:48], False)

    for copy in z_halo:
        copy.wait()

    @pl.when(mp > 0)
    def _():
        wait_halo(halo_recv, 0)
        wait_halo(halo_send, 1)

    @pl.when(mp < spans - 1)
    def _():
        wait_halo(halo_send, 0)

    @pl.when(mp == 0)
    def _():
        yh[0] = jnp.zeros((8, 16, 128), F32)

    @pl.when(mp == spans - 1)
    def _():
        yh[1] = jnp.zeros((8, 16, 128), F32)

    below, above = me > 0, me < GROUPS - 1
    xs = iota((8, 16, 128), 1)
    edge = jnp.where(lane % 2 == 0, pltpu.roll(yh[1], 126, 2), yh[0])
    for s in range(NS):
        cells = sp[s]
        ends = pltpu.roll(edge, 127 - 2 * s, 2)
        zdown = jnp.concatenate([jnp.where(below, zh[0, s], 0.0)[None], cells[:-1]], axis=0)
        zup = jnp.concatenate([cells[1:], jnp.where(above, zh[1, s], 0.0)[None]], axis=0)
        xdown = jnp.where(xs == 0, 0.0, pltpu.roll(cells, 1, 1))
        xup = jnp.where(xs == 15, 0.0, pltpu.roll(cells, 15, 1))
        ydown = jnp.where(lane == 0, ends, pltpu.roll(cells, 1, 2))
        yup = jnp.where(lane == 127, ends, pltpu.roll(cells, 127, 2))
        spread[s] = zup + zdown + xup + xdown + yup + ydown - 6.0 * cells

    for d in range(1, spans):

        @pl.when(mp >= d)
        def _():
            wait_share(share_recv, mp - d)
            wait_share(share_send, mp - d)

        @pl.when(mp + d < spans)
        def _():
            wait_share(share_send, mp + d)

    owed = share[0]
    for g in range(1, spans):
        owed = owed + share[g]
    here = jnp.where(lane2 == mp, owed, 0.0)
    load[...] = jnp.sum(here, axis=1, keepdims=True).astype(jnp.int32)
    load_copy = pltpu.make_async_copy(load, load_out, hist_sem)
    load_copy.start()

    peaks = []
    for z in range(8):
        wide = jnp.broadcast_to(levels[z], (16, 16))
        eye = iota((16, 16), 0) == iota((16, 16), 1)
        kind = jnp.sum(jnp.where(eye, wide.astype(F32), 0.0), axis=1, keepdims=True)
        peaks.append(jnp.where(kind == 0, 1.5, jnp.where(kind == 1, 4.0, jnp.where(kind == 2, 9.0, 19.0))))
    peak = jnp.concatenate(peaks, axis=0).astype(F32)

    for event in events[48:]:
        arrive(*event)
    filter_part(events[48:], False)

    thick = 1.0 + peak * acc[0, :, 0:128]
    stretch = 0.02 * thick
    damp = 4.0 / thick
    for s in range(NS):
        k, half = (s + 1) // 2, (s + 1) % 2
        fine = acc[k, :, 128 * half : 128 * half + 128]
        value = sp[s].reshape(128, 128) + stretch * spread[s].reshape(128, 128) + fine * damp
        out[s] = value.reshape(8, 16, 128)
    load_copy.wait()
    for c in range(CHUNKS):
        sent = rate.at[c, pl.ds(0, GROUPS - 1)]
        pltpu.make_async_copy(sent, sent, send_sem).wait()


def deliver(out, load, out_hbm, load_hbm, sems):
    copies = [
        pltpu.make_async_copy(out, out_hbm, sems.at[0]),
        pltpu.make_async_copy(load, load_hbm, sems.at[1]),
    ]
    for copy in copies:
        copy.start()
    for copy in copies:
        copy.wait()


def shards(spans, species, history, flame_tiles, owners, orders, substeps, levels, mechanism):
    states = jnp.transpose(history, (0, 1, 3, 4, 2, 5)).reshape(3, NS, 32, 128)
    vmem = pl.BlockSpec(memory_space=pltpu.VMEM)
    anywhere = pl.BlockSpec(memory_space=pl.ANY)
    results = (
        jax.ShapeDtypeStruct(species.shape, F32),
        jax.ShapeDtypeStruct((1, 1), jnp.int32),
    )
    out, load = pl.pallas_call(
        functools.partial(kernel, spans),
        out_shape=(pltpu.VMEM(species.shape, F32), results[1]),
        in_specs=[pl.BlockSpec(memory_space=pltpu.SMEM), anywhere, anywhere] + [vmem] * 5,
        out_specs=(vmem, anywhere),
        scratch_shapes=[
            pltpu.VMEM((1, 1), jnp.int32),
            pltpu.VMEM((3, NS, 32, 128), F32),
            pltpu.VMEM((NS, 8, 16, 128), F32),
            pltpu.VMEM((CHUNKS, GROUPS, ROWS, 128), F32),
            pltpu.VMEM((spans, 1, 128), F32),
            pltpu.VMEM((9, 32, 128), F32),
            pltpu.VMEM((2, NS, 16, 128), F32),
            pltpu.VMEM((2, 8, 16, 128), F32),
            pltpu.VMEM((8, 16, 128), F32),
            pltpu.VMEM((NS, 8, 16, 128), F32),
            pltpu.VMEM((5, 128, 256), F32),
            pltpu.SemaphoreType.DMA,
            pltpu.SemaphoreType.DMA,
            pltpu.SemaphoreType.DMA,
            pltpu.SemaphoreType.DMA((CHUNKS, GROUPS)),
            pltpu.SemaphoreType.DMA((spans,)),
            pltpu.SemaphoreType.DMA((spans,)),
            pltpu.SemaphoreType.DMA((4,)),
            pltpu.SemaphoreType.DMA((4,)),
        ],
        compiler_params=pltpu.CompilerParams(
            collective_id=0, has_side_effects=True
        ),
    )(
        mechanism,
        species,
        states,
        flame_tiles.reshape(1, 32),
        owners.reshape(1, 32),
        orders.reshape(1, 32),
        substeps.reshape(1, 32),
        jnp.transpose(levels, (0, 2, 1)),
    )
    return pl.pallas_call(
        deliver,
        out_shape=results,
        in_specs=[anywhere, anywhere],
        out_specs=(anywhere, anywhere),
        scratch_shapes=[pltpu.SemaphoreType.DMA((2,))],
        compiler_params=pltpu.CompilerParams(vmem_limit_bytes=2**20),
    )(out, load)


def solution(mesh):
    in_specs = (
        P(None, "stream", None, "span"),
        P("stream", "span", None, None, None, None),
        P("stream", "span", None),
        P("stream", "span", None, None),
        P("stream", "span", None),
        P("stream", "span", None),
        P("stream", None, "span"),
        P(),
    )
    out_specs = (P(None, "stream", None, "span"), P("stream", "span"))
    return jax.shard_map(
        functools.partial(shards, mesh.shape["span"]),
        mesh=mesh,
        in_specs=in_specs,
        out_specs=out_specs,
        check_vma=False,
    )
```

```python
import functools

import jax
import jax.numpy as jnp
from jax import lax
from jax.experimental import pallas as pl
from jax.experimental.pallas import tpu as pltpu
from jax.sharding import PartitionSpec as P

MESH = pl.DeviceIdType.MESH
F32 = jnp.float32
BF16 = jnp.bfloat16
SUBMAX = 8
NS = 9
SIDE = 4
GROUPS = SIDE * SIDE
CHUNKS = 4
STEPS = (
    (2, 2), (1, 2), (2, 1), (3, 2), (2, 3), (1, 1), (3, 3), (1, 3),
    (3, 1), (0, 2), (2, 0), (0, 1), (1, 0), (0, 3), (3, 0), (0, 0),
)


def iota(shape, dim):
    return lax.broadcasted_iota(jnp.int32, shape, dim)


def by_order(order, one, two, three):
    return jnp.where(order == 1, F32(one), jnp.where(order == 2, F32(two), F32(three)))


def column(row, size):
    wide = jnp.broadcast_to(row.astype(F32), (size, size))
    eye = iota((size, size), 0) == iota((size, size), 1)
    return jnp.sum(jnp.where(eye, wide, 0.0), axis=1, keepdims=True)


def kernel(
    spans,
    mech,
    species_hbm,
    history_hbm,
    tiles,
    owners,
    orders,
    steps,
    levels,
    out,
    load_out,
    load,
    hist,
    sp,
    rate,
    go_out,
    go_in,
    back_out,
    back_in,
    share,
    coef,
    zh,
    yh,
    pack,
    spread,
    hist_sem,
    sp_sem,
    go_send,
    go_recv,
    back_send,
    back_recv,
    share_send,
    share_recv,
    halo_send,
    halo_recv,
):
    me = lax.axis_index("stream")
    mp = lax.axis_index("span")
    sy, sx = me // SIDE, me % SIDE

    hist_copy = pltpu.make_async_copy(history_hbm, hist, hist_sem)
    hist_copy.start()
    sp_copy = pltpu.make_async_copy(species_hbm, sp, sp_sem)
    sp_copy.start()

    def at(dy, dx):
        return ((sy + dy + SIDE) % SIDE) * SIDE + (sx + dx + SIDE) % SIDE

    after, before = (me + 1) % GROUPS, (me + GROUPS - 1) % GROUPS
    barrier = pltpu.get_barrier_semaphore()
    for d in range(1, GROUPS):
        pl.semaphore_signal(barrier, inc=1, device_id={"stream": (me + d) % GROUPS}, device_id_type=MESH)
    for d in range(1, spans):

        @pl.when(mp + d < spans)
        def _():
            pl.semaphore_signal(barrier, inc=1, device_id={"span": mp + d}, device_id_type=MESH)

    order = jnp.broadcast_to(column(orders[...], 32), (32, 128))
    count = column(steps[...], 32)
    tile = column(tiles[...], 32)
    owner = column(owners[...], 32)
    coef[0] = by_order(order, 1.0, 2.0, 3.0)
    coef[1] = by_order(order, 0.0, -1.0, -3.0)
    coef[2] = by_order(order, 0.0, 0.0, 1.0)
    coef[3] = by_order(order, 1.0, 4.0 / 3.0, 18.0 / 11.0)
    coef[4] = by_order(order, 0.0, -1.0 / 3.0, -9.0 / 11.0)
    coef[5] = by_order(order, 0.0, 0.0, 2.0 / 11.0)
    coef[6] = by_order(order, 0.5, 0.5 * 2.0 / 3.0, 0.5 * 6.0 / 11.0)
    count_b = jnp.broadcast_to(count, (32, 128))
    coef[7] = count_b
    coef[8] = 1.0 / jnp.maximum(count_b, 1.0)

    def place(s, c):
        return s // 4, pl.ds(pl.multiple_of(32 * ((s + me) % 4) + 8 * c, 8), 8)

    cell_of = jnp.broadcast_to(tile + (128 * me).astype(F32), (32, 128))
    for c in range(CHUNKS):
        block, rows = place(NS, c)
        rate[block, rows, :] = cell_of[8 * c : 8 * c + 8]
        for s in (10, 11):
            block, rows = place(s, c)
            rate[block, rows, :] = jnp.zeros((8, 128), F32)
    lane32 = iota((32, 128), 1).astype(F32)
    share[mp] = jnp.sum(jnp.where(owner == lane32, count_b, 0.0), axis=0, keepdims=True)

    def chemistry(c):
        rows = slice(8 * c, 8 * c + 8)
        p1, p2, p3, a1, a2, a3, hb, cnt, inv = [coef[k, rows, :] for k in range(9)]
        h1, h2, h3 = [tuple(hist[m, s, rows, :] for s in range(NS)) for m in range(3)]

        def substep(n, carry):
            h1, h2, h3, last = carry
            guess = [p1 * h1[s] + p2 * h2[s] + p3 * h3[s] for s in range(NS)]
            active = cnt > n.astype(F32)
            fresh = []
            done = []
            for s in range(NS):
                total = mech[s, 0] * guess[0]
                for t in range(1, NS):
                    total = total + mech[s, t] * guess[t]
                y = a1 * h1[s] + a2 * h2[s] + a3 * h3[s] + hb * jnp.tanh(total)
                fresh.append(y)
                done.append(jnp.where(active, y, last[s]))
            return tuple(fresh), h1, h2, tuple(done)

        _, _, _, last = lax.fori_loop(0, SUBMAX, substep, (h1, h2, h3, h1))
        for s in range(NS):
            block, spot = place(s, c)
            rate[block, spot, :] = (last[s] - hist[0, s, rows, :]) * inv

    hist_copy.wait()
    for c in range(CHUNKS):
        chemistry(c)
    for b in range(3):
        go_out[:, b] = jnp.transpose(rate[b]).reshape(GROUPS, 8, 128)
    pl.semaphore_wait(barrier, GROUPS - 1 + mp)

    def send(source, target, dst, out_sem, in_sem):
        pltpu.make_async_remote_copy(
            src_ref=source.at[dst],
            dst_ref=target.at[me],
            send_sem=out_sem,
            recv_sem=in_sem.at[me],
            device_id={"stream": dst},
            device_id_type=MESH,
        ).start()

    peers = [at(dy, dx) for dy, dx in STEPS]
    for peer in peers[:-1]:
        send(go_out, go_in, peer, go_send, go_recv)
    go_in[me] = go_out[me]

    sp_copy.wait()
    z_halo = [
        pltpu.make_async_remote_copy(
            sp.at[:, 7], zh.at[0], halo_send.at[0], halo_recv.at[0], device_id={"stream": after}, device_id_type=MESH
        ),
        pltpu.make_async_remote_copy(
            sp.at[:, 0], zh.at[1], halo_send.at[1], halo_recv.at[1], device_id={"stream": before}, device_id_type=MESH
        ),
    ]
    for copy in z_halo:
        copy.start()
    lane = iota((8, 16, 128), 2)
    packed = jnp.zeros((8, 16, 128), F32)
    for s in range(NS):
        turned = pltpu.roll(sp[s], 2 * s + 2, 2)
        packed = jnp.where((lane == 2 * s + 1) | (lane == 2 * s + 2), turned, packed)
    pack[...] = packed

    def send_share(dst):
        pltpu.make_async_remote_copy(
            share.at[mp], share.at[mp], share_send.at[dst], share_recv.at[mp], device_id={"span": dst}, device_id_type=MESH
        ).start()

    def wait_share(sem, k):
        pltpu.make_async_copy(share.at[k], share.at[k], sem.at[k]).wait()

    def halo_copy(slot, dst):
        return pltpu.make_async_remote_copy(
            pack, yh.at[slot], halo_send.at[2 + slot], halo_recv.at[2 + slot], device_id={"span": dst}, device_id_type=MESH
        )

    def wait_halo(sem, slot):
        pltpu.make_async_copy(yh.at[slot], yh.at[slot], sem.at[2 + slot]).wait()

    @pl.when(mp > 0)
    def _():
        halo_copy(1, mp - 1).start()

    for d in range(1, spans):

        @pl.when(mp >= d)
        def _():
            send_share(mp - d)

    for peer in peers[:-1]:
        pltpu.make_async_copy(go_in.at[peer], go_in.at[peer], go_recv.at[peer]).wait()
    quarter = iota((8, 128), 1) // 32

    def gathered(s, q):
        block, k = s // 4, s % 4
        value = go_in[4 * q, block]
        for i in range(1, 4):
            value = jnp.where(quarter == (k + i) % 4, go_in[4 * q + i, block], value)
        return value if k == 0 else pltpu.roll(value, 128 - 32 * k, 1)

    def line(s):
        return jnp.concatenate([gathered(s, q) for q in range(4)], axis=1)

    values = [line(s) for s in range(NS)]
    power = values[0] * values[0]
    for s in range(1, NS):
        power = power + values[s] * values[s]
    power = power * (1.0 / NS)
    values = jnp.concatenate(values + [power / (power + 1.0)], axis=0)
    high = values.astype(BF16)
    low = (values - high.astype(F32)).astype(BF16)
    left = jnp.concatenate([high, low, high], axis=1)

    cells = line(NS)[0:1]
    from_z = jnp.floor(cells * (1.0 / 16.0))
    from_x = cells - 16.0 * from_z
    row = iota((128, 512), 0)
    row_z = (row // 16).astype(F32) * (1.0 / 16.0)
    same_x = (row % 16).astype(F32) == from_x
    from_z = from_z * (1.0 / 16.0)

    def weights(dst):
        offset = row_z - (from_z - 0.5 * dst.astype(F32))
        weight = jnp.where(same_x, jnp.exp(-0.5 * offset * offset), 0.0)
        high = weight.astype(BF16)
        low = (weight - high.astype(F32)).astype(BF16)
        return jnp.concatenate([high, high, low], axis=1)

    for n in range(0, GROUPS, 2):
        right = jnp.concatenate([weights(dst) for dst in peers[n : n + 2]], axis=0)
        part = lax.dot_general(left, right, (((1,), (1,)), ((), ())), preferred_element_type=F32)
        for k, dst in enumerate(peers[n : n + 2]):
            piece = part[:, 128 * k : 128 * k + 128]
            if n + k < GROUPS - 1:
                back_out[dst] = piece
                send(back_out, back_in, dst, back_send, back_recv)
            else:
                back_in[me] = piece

    @pl.when(mp < spans - 1)
    def _():
        wait_halo(halo_recv, 1)
        halo_copy(0, mp + 1).start()

    for d in range(1, spans):

        @pl.when(mp + d < spans)
        def _():
            wait_share(share_recv, mp + d)
            send_share(mp + d)

    for copy in z_halo:
        copy.wait()

    @pl.when(mp > 0)
    def _():
        wait_halo(halo_recv, 0)
        wait_halo(halo_send, 1)

    @pl.when(mp < spans - 1)
    def _():
        wait_halo(halo_send, 0)

    @pl.when(mp == 0)
    def _():
        yh[0] = jnp.zeros((8, 16, 128), F32)

    @pl.when(mp == spans - 1)
    def _():
        yh[1] = jnp.zeros((8, 16, 128), F32)

    below, above = me > 0, me < GROUPS - 1
    xs = iota((8, 16, 128), 1)
    edge = jnp.where(lane % 2 == 0, pltpu.roll(yh[1], 126, 2), yh[0])
    for s in range(NS):
        cells = sp[s]
        ends = pltpu.roll(edge, 127 - 2 * s, 2)
        zdown = jnp.concatenate([jnp.where(below, zh[0, s], 0.0)[None], cells[:-1]], axis=0)
        zup = jnp.concatenate([cells[1:], jnp.where(above, zh[1, s], 0.0)[None]], axis=0)
        xdown = jnp.where(xs == 0, 0.0, pltpu.roll(cells, 1, 1))
        xup = jnp.where(xs == 15, 0.0, pltpu.roll(cells, 15, 1))
        ydown = jnp.where(lane == 0, ends, pltpu.roll(cells, 1, 2))
        yup = jnp.where(lane == 127, ends, pltpu.roll(cells, 127, 2))
        spread[s] = zup + zdown + xup + xdown + yup + ydown - 6.0 * cells

    for d in range(1, spans):

        @pl.when(mp >= d)
        def _():
            wait_share(share_recv, mp - d)
            wait_share(share_send, mp - d)

        @pl.when(mp + d < spans)
        def _():
            wait_share(share_send, mp + d)

    lane2 = iota((1, 128), 1)
    owed = share[0]
    for g in range(1, spans):
        owed = owed + share[g]
    here = jnp.where(lane2 == mp, owed, 0.0)
    load[...] = jnp.sum(here, axis=1, keepdims=True).astype(jnp.int32)
    load_copy = pltpu.make_async_copy(load, load_out, hist_sem)
    load_copy.start()

    peaks = []
    for z in range(8):
        wide = jnp.broadcast_to(levels[z], (16, 16))
        eye = iota((16, 16), 0) == iota((16, 16), 1)
        kind = jnp.sum(jnp.where(eye, wide.astype(F32), 0.0), axis=1, keepdims=True)
        peaks.append(jnp.where(kind == 0, 1.5, jnp.where(kind == 1, 4.0, jnp.where(kind == 2, 9.0, 19.0))))
    peak = jnp.concatenate(peaks, axis=0).astype(F32)

    cell_z = (iota((128, 128), 0) // 16 + 8 * me).astype(F32)
    offset = (cell_z - iota((128, 128), 1).astype(F32)) * (1.0 / 16.0)
    norm = 1.0 / jnp.sum(jnp.exp(-0.5 * offset * offset), axis=1, keepdims=True)
    peak = peak * norm
    norm = 4.0 * norm

    for peer in peers[:-1]:
        pltpu.make_async_copy(back_in.at[peer], back_in.at[peer], back_recv.at[peer]).wait()

    def smoothed(s):
        return jnp.transpose(back_in[:, 8 * s : 8 * s + 8, :].reshape(128, 128))

    thick = 1.0 + peak * smoothed(NS)
    stretch = 0.02 * thick
    damp = norm / thick
    for s in range(NS):
        value = sp[s].reshape(128, 128) + stretch * spread[s].reshape(128, 128) + smoothed(s) * damp
        out[s] = value.reshape(8, 16, 128)
    load_copy.wait()
    for buffer, sem in ((go_out, go_send), (back_out, back_send)):
        sent = buffer.at[pl.ds(0, GROUPS - 1)]
        pltpu.make_async_copy(sent, sent, sem).wait()


def deliver(out, load, out_hbm, load_hbm, sems):
    copies = [
        pltpu.make_async_copy(out, out_hbm, sems.at[0]),
        pltpu.make_async_copy(load, load_hbm, sems.at[1]),
    ]
    for copy in copies:
        copy.start()
    for copy in copies:
        copy.wait()


def shards(spans, species, history, flame_tiles, owners, orders, substeps, levels, mechanism):
    states = jnp.transpose(history, (0, 1, 3, 4, 2, 5)).reshape(3, NS, 32, 128)
    vmem = pl.BlockSpec(memory_space=pltpu.VMEM)
    anywhere = pl.BlockSpec(memory_space=pl.ANY)
    results = (
        jax.ShapeDtypeStruct(species.shape, F32),
        jax.ShapeDtypeStruct((1, 1), jnp.int32),
    )
    out, load = pl.pallas_call(
        functools.partial(kernel, spans),
        out_shape=(pltpu.VMEM(species.shape, F32), results[1]),
        in_specs=[pl.BlockSpec(memory_space=pltpu.SMEM), anywhere, anywhere] + [vmem] * 5,
        out_specs=(vmem, anywhere),
        scratch_shapes=[
            pltpu.VMEM((1, 1), jnp.int32),
            pltpu.VMEM((3, NS, 32, 128), F32),
            pltpu.VMEM((NS, 8, 16, 128), F32),
            pltpu.VMEM((3, 128, 128), F32),
            pltpu.VMEM((GROUPS, 3, 8, 128), F32),
            pltpu.VMEM((GROUPS, 3, 8, 128), F32),
            pltpu.VMEM((GROUPS, 80, 128), F32),
            pltpu.VMEM((GROUPS, 80, 128), F32),
            pltpu.VMEM((spans, 1, 128), F32),
            pltpu.VMEM((9, 32, 128), F32),
            pltpu.VMEM((2, NS, 16, 128), F32),
            pltpu.VMEM((2, 8, 16, 128), F32),
            pltpu.VMEM((8, 16, 128), F32),
            pltpu.VMEM((NS, 8, 16, 128), F32),
            pltpu.SemaphoreType.DMA,
            pltpu.SemaphoreType.DMA,
            pltpu.SemaphoreType.DMA,
            pltpu.SemaphoreType.DMA((GROUPS,)),
            pltpu.SemaphoreType.DMA,
            pltpu.SemaphoreType.DMA((GROUPS,)),
            pltpu.SemaphoreType.DMA((spans,)),
            pltpu.SemaphoreType.DMA((spans,)),
            pltpu.SemaphoreType.DMA((4,)),
            pltpu.SemaphoreType.DMA((4,)),
        ],
        compiler_params=pltpu.CompilerParams(
            collective_id=0, has_side_effects=True
        ),
    )(
        mechanism,
        species,
        states,
        flame_tiles.reshape(1, 32),
        owners.reshape(1, 32),
        orders.reshape(1, 32),
        substeps.reshape(1, 32),
        jnp.transpose(levels, (0, 2, 1)),
    )
    return pl.pallas_call(
        deliver,
        out_shape=results,
        in_specs=[anywhere, anywhere],
        out_specs=(anywhere, anywhere),
        scratch_shapes=[pltpu.SemaphoreType.DMA((2,))],
        compiler_params=pltpu.CompilerParams(vmem_limit_bytes=2**20),
    )(out, load)


def solution(mesh):
    in_specs = (
        P(None, "stream", None, "span"),
        P("stream", "span", None, None, None, None),
        P("stream", "span", None),
        P("stream", "span", None, None),
        P("stream", "span", None),
        P("stream", "span", None),
        P("stream", None, "span"),
        P(),
    )
    out_specs = (P(None, "stream", None, "span"), P("stream", "span"))
    return jax.shard_map(
        functools.partial(shards, mesh.shape["span"]),
        mesh=mesh,
        in_specs=in_specs,
        out_specs=out_specs,
        check_vma=False,
    )
```

```python
import functools

import jax
import jax.numpy as jnp
from jax import lax
from jax.experimental import pallas as pl
from jax.experimental.pallas import tpu as pltpu
from jax.sharding import PartitionSpec as P

MESH = pl.DeviceIdType.MESH
F32 = jnp.float32
BF16 = jnp.bfloat16
SUBMAX = 8
NS = 9
SIDE = 4
GROUPS = SIDE * SIDE
CHUNKS = 4
FIRST = ((2, 2), (1, 2), (2, 1), (3, 2), (2, 3), (1, 1), (3, 3), (0, 0))
OTHERS = ((1, 3), (3, 1), (0, 2), (2, 0), (0, 1), (1, 0), (0, 3), (3, 0))


def iota(shape, dim):
    return lax.broadcasted_iota(jnp.int32, shape, dim)


def by_order(order, one, two, three):
    return jnp.where(order == 1, F32(one), jnp.where(order == 2, F32(two), F32(three)))


def column(row, size):
    wide = jnp.broadcast_to(row.astype(F32), (size, size))
    eye = iota((size, size), 0) == iota((size, size), 1)
    return jnp.sum(jnp.where(eye, wide, 0.0), axis=1, keepdims=True)


def kernel(
    spans,
    mech_hbm,
    species_hbm,
    history_hbm,
    tiles_hbm,
    owners_hbm,
    orders_hbm,
    steps_hbm,
    levels_hbm,
    out,
    mech,
    tiles,
    owners,
    orders,
    steps,
    levels,
    hist,
    sp,
    rate,
    meta,
    wts,
    left,
    go_out,
    go_in,
    back_out,
    back_in,
    share,
    coef,
    zh,
    yh,
    pack,
    spread,
    table_sem,
    hist_sem,
    sp_sem,
    meta_send,
    meta_recv,
    go_send,
    go_recv,
    back_send,
    back_recv,
    share_send,
    share_recv,
    halo_send,
    halo_recv,
):
    me = lax.axis_index("stream")
    mp = lax.axis_index("span")
    sy, sx = me // SIDE, me % SIDE

    table_copies = [
        pltpu.make_async_copy(source, target, table_sem.at[k])
        for k, (source, target) in enumerate(
            (
                (orders_hbm, orders),
                (steps_hbm, steps),
                (tiles_hbm, tiles),
                (owners_hbm, owners),
                (mech_hbm, mech),
                (levels_hbm, levels),
            )
        )
    ]
    for copy in table_copies:
        copy.start()
    hist_copy = pltpu.make_async_copy(history_hbm, hist, hist_sem)
    hist_copy.start()
    sp_copy = pltpu.make_async_copy(species_hbm, sp, sp_sem)
    sp_copy.start()

    def at(dy, dx):
        return ((sy + dy + SIDE) % SIDE) * SIDE + (sx + dx + SIDE) % SIDE

    after, before = (me + 1) % GROUPS, (me + GROUPS - 1) % GROUPS
    barrier = pltpu.get_barrier_semaphore()
    for d in range(1, GROUPS):
        pl.semaphore_signal(barrier, inc=1, device_id={"stream": (me + d) % GROUPS}, device_id_type=MESH)
    for d in range(1, spans):

        @pl.when(mp + d < spans)
        def _():
            pl.semaphore_signal(barrier, inc=1, device_id={"span": mp + d}, device_id_type=MESH)

    for copy in table_copies:
        copy.wait()
    order = jnp.broadcast_to(column(orders[...], 32), (32, 128))
    count = column(steps[...], 32)
    tile = column(tiles[...], 32)
    owner = column(owners[...], 32)
    coef[0] = by_order(order, 1.0, 2.0, 3.0)
    coef[1] = by_order(order, 0.0, -1.0, -3.0)
    coef[2] = by_order(order, 0.0, 0.0, 1.0)
    coef[3] = by_order(order, 1.0, 4.0 / 3.0, 18.0 / 11.0)
    coef[4] = by_order(order, 0.0, -1.0 / 3.0, -9.0 / 11.0)
    coef[5] = by_order(order, 0.0, 0.0, 2.0 / 11.0)
    coef[6] = by_order(order, 0.5, 0.5 * 2.0 / 3.0, 0.5 * 6.0 / 11.0)
    count_b = jnp.broadcast_to(count, (32, 128))
    coef[7] = count_b
    coef[8] = 1.0 / jnp.maximum(count_b, 1.0)

    def place(s, c):
        return s // 4, pl.ds(pl.multiple_of(32 * ((s + me) % 4) + 8 * c, 8), 8)

    cell_of = jnp.broadcast_to(tile + (128 * me).astype(F32), (32, 128))
    mine = iota((32, 128), 1) == iota((32, 128), 0) + 32 * (me % 4)
    meta[me] = jnp.sum(jnp.where(mine, cell_of, 0.0), axis=0, keepdims=True)
    for c in range(CHUNKS):
        for s in (9, 10, 11):
            block, rows = place(s, c)
            rate[block, rows, :] = jnp.zeros((8, 128), F32)
    lane32 = iota((32, 128), 1).astype(F32)
    share[mp] = jnp.sum(jnp.where(owner == lane32, count_b, 0.0), axis=0, keepdims=True)

    def chemistry(c):
        rows = slice(8 * c, 8 * c + 8)
        p1, p2, p3, a1, a2, a3, hb, cnt, inv = [coef[k, rows, :] for k in range(9)]
        h1, h2, h3 = [tuple(hist[m, s, rows, :] for s in range(NS)) for m in range(3)]

        last = h1
        for n in range(SUBMAX):
            guess = [p1 * h1[s] + p2 * h2[s] + p3 * h3[s] for s in range(NS)]
            active = cnt > F32(n)
            fresh = []
            done = []
            for s in range(NS):
                total = mech[s, 0] * guess[0]
                for t in range(1, NS):
                    total = total + mech[s, t] * guess[t]
                y = a1 * h1[s] + a2 * h2[s] + a3 * h3[s] + hb * jnp.tanh(total)
                fresh.append(y)
                done.append(jnp.where(active, y, last[s]))
            h1, h2, h3, last = fresh, h1, h2, done
        for s in range(NS):
            block, spot = place(s, c)
            rate[block, spot, :] = (last[s] - hist[0, s, rows, :]) * inv

    hist_copy.wait()
    for c in range(CHUNKS):
        chemistry(c)
    for b in range(3):
        go_out[:, b] = jnp.transpose(rate[b]).reshape(GROUPS, 8, 128)
    pl.semaphore_wait(barrier, GROUPS - 1 + mp)

    def send(source, target, dst, out_sem, in_sem):
        pltpu.make_async_remote_copy(
            src_ref=source,
            dst_ref=target.at[me],
            send_sem=out_sem,
            recv_sem=in_sem,
            device_id={"stream": dst},
            device_id_type=MESH,
        ).start()

    first = [at(dy, dx) for dy, dx in FIRST]
    others = [at(dy, dx) for dy, dx in OTHERS]
    peers = first[:-1] + others
    for peer in peers:
        send(meta.at[me], meta, peer, meta_send, meta_recv)
    for peer in peers:
        send(go_out.at[peer], go_in, peer, go_send, go_recv.at[me])
    go_in[me] = go_out[me]

    sp_copy.wait()
    z_halo = [
        pltpu.make_async_remote_copy(
            sp.at[:, 7], zh.at[0], halo_send.at[0], halo_recv.at[0], device_id={"stream": after}, device_id_type=MESH
        ),
        pltpu.make_async_remote_copy(
            sp.at[:, 0], zh.at[1], halo_send.at[1], halo_recv.at[1], device_id={"stream": before}, device_id_type=MESH
        ),
    ]
    for copy in z_halo:
        copy.start()
    lane = iota((8, 16, 128), 2)
    packed = jnp.zeros((8, 16, 128), F32)
    for s in range(NS):
        turned = pltpu.roll(sp[s], 2 * s + 2, 2)
        packed = jnp.where((lane == 2 * s + 1) | (lane == 2 * s + 2), turned, packed)
    pack[...] = packed

    def send_share(dst):
        pltpu.make_async_remote_copy(
            share.at[mp], share.at[mp], share_send.at[dst], share_recv.at[mp], device_id={"span": dst}, device_id_type=MESH
        ).start()

    def wait_share(sem, k):
        pltpu.make_async_copy(share.at[k], share.at[k], sem.at[k]).wait()

    def halo_copy(slot, dst):
        return pltpu.make_async_remote_copy(
            pack, yh.at[slot], halo_send.at[2 + slot], halo_recv.at[2 + slot], device_id={"span": dst}, device_id_type=MESH
        )

    def wait_halo(sem, slot):
        pltpu.make_async_copy(yh.at[slot], yh.at[slot], sem.at[2 + slot]).wait()

    @pl.when(mp > 0)
    def _():
        halo_copy(1, mp - 1).start()

    for d in range(1, spans):

        @pl.when(mp >= d)
        def _():
            send_share(mp - d)

    some = meta.at[pl.ds(0, GROUPS - 1)]
    pltpu.make_async_copy(some, some, meta_recv).wait()
    cells = jnp.concatenate([meta[4 * q] + meta[4 * q + 1] + meta[4 * q + 2] + meta[4 * q + 3] for q in range(4)], axis=1)
    from_z = jnp.floor(cells * (1.0 / 16.0))
    from_x = cells - 16.0 * from_z
    row = iota((128, 512), 0)
    row_z = (row // 16).astype(F32) * (1.0 / 16.0)
    same_x = (row % 16).astype(F32) == from_x
    from_z = from_z * (1.0 / 16.0)

    def weights(dst):
        offset = row_z - (from_z - 0.5 * dst.astype(F32))
        weight = jnp.where(same_x, jnp.exp(-0.5 * offset * offset), 0.0)
        high = weight.astype(BF16)
        low = (weight - high.astype(F32)).astype(BF16)
        return jnp.concatenate([high, high, low], axis=1)

    for n, dst in enumerate(first):
        wts[n] = weights(dst)

    for peer in peers:
        pltpu.make_async_copy(go_in.at[peer], go_in.at[peer], go_recv.at[peer]).wait()
    quarter = iota((8, 128), 1) // 32

    def gathered(s, q):
        block, k = s // 4, s % 4
        value = go_in[4 * q, block]
        for i in range(1, 4):
            value = jnp.where(quarter == (k + i) % 4, go_in[4 * q + i, block], value)
        return value if k == 0 else pltpu.roll(value, 128 - 32 * k, 1)

    values = [jnp.concatenate([gathered(s, q) for q in range(4)], axis=1) for s in range(NS)]
    power = values[0] * values[0]
    for s in range(1, NS):
        power = power + values[s] * values[s]
    power = power * (1.0 / NS)
    values = jnp.concatenate(values + [power / (power + 1.0)], axis=0)
    high = values.astype(BF16)
    low = (values - high.astype(F32)).astype(BF16)
    left[...] = jnp.concatenate([high, low, high], axis=1)

    def product(right):
        return lax.dot_general(left[...], right, (((1,), (1,)), ((), ())), preferred_element_type=F32)

    def give(piece, dst):
        back_out[dst] = piece
        send(back_out.at[dst], back_in, dst, back_send, back_recv.at[me])

    for n in range(0, 8, 2):
        part = product(wts[n : n + 2].reshape(256, 1536))
        give(part[:, :128], first[n])
        if n + 1 < 7:
            give(part[:, 128:], first[n + 1])
        else:
            back_in[me] = part[:, 128:]

    steps_y = sum(dy << (2 * k) for k, (dy, _) in enumerate(OTHERS))
    steps_x = sum(dx << (2 * k) for k, (_, dx) in enumerate(OTHERS))

    def two_others(n, _):
        pair = []
        for k in range(2):
            shift = 4 * n + 2 * k
            dy = lax.shift_right_logical(jnp.int32(steps_y), shift) & 3
            dx = lax.shift_right_logical(jnp.int32(steps_x), shift) & 3
            pair.append(at(dy, dx))
        part = product(jnp.concatenate([weights(dst) for dst in pair], axis=0))
        for k, dst in enumerate(pair):
            give(part[:, 128 * k : 128 * k + 128], dst)
        return 0

    lax.fori_loop(0, 4, two_others, 0)

    @pl.when(mp < spans - 1)
    def _():
        wait_halo(halo_recv, 1)
        halo_copy(0, mp + 1).start()

    for d in range(1, spans):

        @pl.when(mp + d < spans)
        def _():
            wait_share(share_recv, mp + d)
            send_share(mp + d)

    for copy in z_halo:
        copy.wait()

    @pl.when(mp > 0)
    def _():
        wait_halo(halo_recv, 0)
        wait_halo(halo_send, 1)

    @pl.when(mp < spans - 1)
    def _():
        wait_halo(halo_send, 0)

    @pl.when(mp == 0)
    def _():
        yh[0] = jnp.zeros((8, 16, 128), F32)

    @pl.when(mp == spans - 1)
    def _():
        yh[1] = jnp.zeros((8, 16, 128), F32)

    below, above = me > 0, me < GROUPS - 1
    xs = iota((8, 16, 128), 1)
    edge = jnp.where(lane % 2 == 0, pltpu.roll(yh[1], 126, 2), yh[0])
    for s in range(NS):
        cells = sp[s]
        ends = pltpu.roll(edge, 127 - 2 * s, 2)
        zdown = jnp.concatenate([jnp.where(below, zh[0, s], 0.0)[None], cells[:-1]], axis=0)
        zup = jnp.concatenate([cells[1:], jnp.where(above, zh[1, s], 0.0)[None]], axis=0)
        xdown = jnp.where(xs == 0, 0.0, pltpu.roll(cells, 1, 1))
        xup = jnp.where(xs == 15, 0.0, pltpu.roll(cells, 15, 1))
        ydown = jnp.where(lane == 0, ends, pltpu.roll(cells, 1, 2))
        yup = jnp.where(lane == 127, ends, pltpu.roll(cells, 127, 2))
        spread[s] = zup + zdown + xup + xdown + yup + ydown - 6.0 * cells

    for d in range(1, spans):

        @pl.when(mp >= d)
        def _():
            wait_share(share_recv, mp - d)
            wait_share(share_send, mp - d)

        @pl.when(mp + d < spans)
        def _():
            wait_share(share_send, mp + d)

    lane2 = iota((1, 128), 1)
    owed = share[0]
    for g in range(1, spans):
        owed = owed + share[g]
    here = jnp.where(lane2 == mp, owed, 0.0)
    out[8 * NS] = jnp.broadcast_to(jnp.sum(here, axis=1, keepdims=True), (16, 128))

    peaks = []
    for z in range(8):
        wide = jnp.broadcast_to(levels[z], (16, 16))
        eye = iota((16, 16), 0) == iota((16, 16), 1)
        kind = jnp.sum(jnp.where(eye, wide.astype(F32), 0.0), axis=1, keepdims=True)
        peaks.append(jnp.where(kind == 0, 1.5, jnp.where(kind == 1, 4.0, jnp.where(kind == 2, 9.0, 19.0))))
    peak = jnp.concatenate(peaks, axis=0).astype(F32)

    cell_z = (iota((128, 128), 0) // 16 + 8 * me).astype(F32)
    offset = (cell_z - iota((128, 128), 1).astype(F32)) * (1.0 / 16.0)
    norm = 1.0 / jnp.sum(jnp.exp(-0.5 * offset * offset), axis=1, keepdims=True)
    peak = peak * norm
    norm = 4.0 * norm

    for peer in peers:
        pltpu.make_async_copy(back_in.at[peer], back_in.at[peer], back_recv.at[peer]).wait()

    def smoothed(s):
        return jnp.transpose(back_in[:, 8 * s : 8 * s + 8, :].reshape(128, 128))

    thick = 1.0 + peak * smoothed(NS)
    stretch = 0.02 * thick
    damp = norm / thick
    for s in range(NS):
        value = sp[s].reshape(128, 128) + stretch * spread[s].reshape(128, 128) + smoothed(s) * damp
        out[8 * s : 8 * s + 8] = value.reshape(8, 16, 128)
    for buffer, sem in ((meta, meta_send), (go_out, go_send), (back_out, back_send)):
        sent = buffer.at[pl.ds(0, GROUPS - 1)]
        pltpu.make_async_copy(sent, sent, sem).wait()


def deliver(both, out_hbm, load_hbm, load, sems):
    cells = both.at[pl.ds(0, 8 * NS)]
    copies = [
        pltpu.make_async_copy(cells, out_hbm, sems.at[0]),
        pltpu.make_async_copy(load, load_hbm, sems.at[1]),
    ]
    copies[0].start()
    load[...] = both[8 * NS, 0:1, 0:1].astype(jnp.int32)
    copies[1].start()
    for copy in copies:
        copy.wait()


def shards(spans, species, history, flame_tiles, owners, orders, substeps, levels, mechanism):
    states = jnp.transpose(history, (0, 1, 3, 4, 2, 5)).reshape(3, NS, 32, 128)
    vmem = pl.BlockSpec(memory_space=pltpu.VMEM)
    anywhere = pl.BlockSpec(memory_space=pl.ANY)
    both = pl.pallas_call(
        functools.partial(kernel, spans),
        out_shape=pltpu.VMEM((8 * NS + 1, 16, 128), F32),
        in_specs=[anywhere] * 8,
        out_specs=vmem,
        scratch_shapes=[
            pltpu.SMEM((NS, NS), F32),
            pltpu.VMEM((1, 32), jnp.int32),
            pltpu.VMEM((1, 32), jnp.int32),
            pltpu.VMEM((1, 32), jnp.int32),
            pltpu.VMEM((1, 32), jnp.int32),
            pltpu.VMEM((8, 1, 16), jnp.int32),
            pltpu.VMEM((3, NS, 32, 128), F32),
            pltpu.VMEM((NS, 8, 16, 128), F32),
            pltpu.VMEM((3, 128, 128), F32),
            pltpu.VMEM((GROUPS, 1, 128), F32),
            pltpu.VMEM((8, 128, 1536), BF16),
            pltpu.VMEM((80, 1536), BF16),
            pltpu.VMEM((GROUPS, 3, 8, 128), F32),
            pltpu.VMEM((GROUPS, 3, 8, 128), F32),
            pltpu.VMEM((GROUPS, 80, 128), F32),
            pltpu.VMEM((GROUPS, 80, 128), F32),
            pltpu.VMEM((spans, 1, 128), F32),
            pltpu.VMEM((9, 32, 128), F32),
            pltpu.VMEM((2, NS, 16, 128), F32),
            pltpu.VMEM((2, 8, 16, 128), F32),
            pltpu.VMEM((8, 16, 128), F32),
            pltpu.VMEM((NS, 8, 16, 128), F32),
            pltpu.SemaphoreType.DMA((6,)),
            pltpu.SemaphoreType.DMA,
            pltpu.SemaphoreType.DMA,
            pltpu.SemaphoreType.DMA,
            pltpu.SemaphoreType.DMA,
            pltpu.SemaphoreType.DMA,
            pltpu.SemaphoreType.DMA((GROUPS,)),
            pltpu.SemaphoreType.DMA,
            pltpu.SemaphoreType.DMA((GROUPS,)),
            pltpu.SemaphoreType.DMA((spans,)),
            pltpu.SemaphoreType.DMA((spans,)),
            pltpu.SemaphoreType.DMA((4,)),
            pltpu.SemaphoreType.DMA((4,)),
        ],
        compiler_params=pltpu.CompilerParams(
            collective_id=0, has_side_effects=True
        ),
    )(
        mechanism,
        species,
        states,
        flame_tiles.reshape(1, 32),
        owners.reshape(1, 32),
        orders.reshape(1, 32),
        substeps.reshape(1, 32),
        jnp.transpose(levels, (0, 2, 1)),
    )
    out, load = pl.pallas_call(
        deliver,
        out_shape=(
            jax.ShapeDtypeStruct((8 * NS, 16, 128), F32),
            jax.ShapeDtypeStruct((1, 1), jnp.int32),
        ),
        in_specs=[vmem],
        out_specs=(anywhere, anywhere),
        scratch_shapes=[pltpu.VMEM((1, 1), jnp.int32), pltpu.SemaphoreType.DMA((2,))],
        compiler_params=pltpu.CompilerParams(vmem_limit_bytes=2**20),
    )(both)
    return out.reshape(species.shape), load


def solution(mesh):
    in_specs = (
        P(None, "stream", None, "span"),
        P("stream", "span", None, None, None, None),
        P("stream", "span", None),
        P("stream", "span", None, None),
        P("stream", "span", None),
        P("stream", "span", None),
        P("stream", None, "span"),
        P(),
    )
    out_specs = (P(None, "stream", None, "span"), P("stream", "span"))
    return jax.shard_map(
        functools.partial(shards, mesh.shape["span"]),
        mesh=mesh,
        in_specs=in_specs,
        out_specs=out_specs,
        check_vma=False,
    )
```

```python
import functools

import jax
import jax.numpy as jnp
from jax import lax
from jax.experimental import pallas as pl
from jax.experimental.pallas import tpu as pltpu
from jax.sharding import PartitionSpec as P

MESH = pl.DeviceIdType.MESH
F32 = jnp.float32
BF16 = jnp.bfloat16
SUBMAX = 8
NS = 9
SIDE = 4
GROUPS = SIDE * SIDE
CHUNKS = 4
FIRST = ((1, 1), (3, 3), (2, 0), (3, 1), (1, 3), (2, 2), (2, 1), (0, 0))
OTHERS = ((2, 3), (1, 0), (1, 2), (3, 2), (3, 0), (0, 2), (0, 1), (0, 3))


def iota(shape, dim):
    return lax.broadcasted_iota(jnp.int32, shape, dim)


def by_order(order, one, two, three):
    return jnp.where(order == 1, F32(one), jnp.where(order == 2, F32(two), F32(three)))


def column(row, size):
    wide = jnp.broadcast_to(row.astype(F32), (size, size))
    eye = iota((size, size), 0) == iota((size, size), 1)
    return jnp.sum(jnp.where(eye, wide, 0.0), axis=1, keepdims=True)


def kernel(
    spans,
    mech_hbm,
    species_hbm,
    history_hbm,
    tiles_hbm,
    owners_hbm,
    orders_hbm,
    steps_hbm,
    levels_hbm,
    out,
    mech,
    tiles,
    owners,
    orders,
    steps,
    levels,
    hist,
    sp,
    rate,
    meta,
    wts,
    left,
    go_out,
    go_in,
    back_out,
    back_in,
    share,
    coef,
    zh,
    yh,
    pack,
    spread,
    table_sem,
    hist_sem,
    sp_sem,
    meta_send,
    meta_recv,
    go_send,
    go_recv,
    back_send,
    back_recv,
    share_send,
    share_recv,
    halo_send,
    halo_recv,
):
    me = lax.axis_index("stream")
    mp = lax.axis_index("span")
    sy, sx = me // SIDE, me % SIDE

    table_copies = [
        pltpu.make_async_copy(source, target, table_sem.at[k])
        for k, (source, target) in enumerate(
            (
                (orders_hbm, orders),
                (steps_hbm, steps),
                (tiles_hbm, tiles),
                (owners_hbm, owners),
                (mech_hbm, mech),
                (levels_hbm, levels),
            )
        )
    ]
    for copy in table_copies:
        copy.start()
    hist_copy = pltpu.make_async_copy(history_hbm, hist, hist_sem)
    hist_copy.start()
    sp_copy = pltpu.make_async_copy(species_hbm, sp, sp_sem)
    sp_copy.start()

    def at(dy, dx):
        return ((sy + dy + SIDE) % SIDE) * SIDE + (sx + dx + SIDE) % SIDE

    after, before = (me + 1) % GROUPS, (me + GROUPS - 1) % GROUPS
    barrier = pltpu.get_barrier_semaphore()
    for d in range(1, GROUPS):
        pl.semaphore_signal(barrier, inc=1, device_id={"stream": (me + d) % GROUPS}, device_id_type=MESH)
    for d in range(1, spans):

        @pl.when(mp + d < spans)
        def _():
            pl.semaphore_signal(barrier, inc=1, device_id={"span": mp + d}, device_id_type=MESH)

    for copy in table_copies:
        copy.wait()
    order = jnp.broadcast_to(column(orders[...], 32), (32, 128))
    count = column(steps[...], 32)
    tile = column(tiles[...], 32)
    owner = column(owners[...], 32)
    coef[0] = by_order(order, 1.0, 2.0, 3.0)
    coef[1] = by_order(order, 0.0, -1.0, -3.0)
    coef[2] = by_order(order, 0.0, 0.0, 1.0)
    coef[3] = by_order(order, 1.0, 4.0 / 3.0, 18.0 / 11.0)
    coef[4] = by_order(order, 0.0, -1.0 / 3.0, -9.0 / 11.0)
    coef[5] = by_order(order, 0.0, 0.0, 2.0 / 11.0)
    coef[6] = by_order(order, 0.5, 0.5 * 2.0 / 3.0, 0.5 * 6.0 / 11.0)
    count_b = jnp.broadcast_to(count, (32, 128))
    coef[7] = count_b
    coef[8] = 1.0 / jnp.maximum(count_b, 1.0)

    def place(s, c):
        return s // 4, pl.ds(pl.multiple_of(32 * ((s + me) % 4) + 8 * c, 8), 8)

    cell_of = jnp.broadcast_to(tile + (128 * me).astype(F32), (32, 128))
    mine = iota((32, 128), 1) == iota((32, 128), 0) + 32 * (me % 4)
    meta[me] = jnp.sum(jnp.where(mine, cell_of, 0.0), axis=0, keepdims=True)
    for c in range(CHUNKS):
        for s in (9, 10, 11):
            block, rows = place(s, c)
            rate[block, rows, :] = jnp.zeros((8, 128), F32)
    lane32 = iota((32, 128), 1).astype(F32)
    share[mp] = jnp.sum(jnp.where(owner == lane32, count_b, 0.0), axis=0, keepdims=True)

    def chemistry(c):
        rows = slice(8 * c, 8 * c + 8)
        p1, p2, p3, a1, a2, a3, hb, cnt, inv = [coef[k, rows, :] for k in range(9)]
        h1, h2, h3 = [tuple(hist[m, s, rows, :] for s in range(NS)) for m in range(3)]

        last = h1
        for n in range(SUBMAX):
            guess = [p1 * h1[s] + p2 * h2[s] + p3 * h3[s] for s in range(NS)]
            active = cnt > F32(n)
            fresh = []
            done = []
            for s in range(NS):
                total = mech[s, 0] * guess[0]
                for t in range(1, NS):
                    total = total + mech[s, t] * guess[t]
                y = a1 * h1[s] + a2 * h2[s] + a3 * h3[s] + hb * jnp.tanh(total)
                fresh.append(y)
                done.append(jnp.where(active, y, last[s]))
            h1, h2, h3, last = fresh, h1, h2, done
        for s in range(NS):
            block, spot = place(s, c)
            rate[block, spot, :] = (last[s] - hist[0, s, rows, :]) * inv

    hist_copy.wait()
    for c in range(CHUNKS):
        chemistry(c)
    for b in range(3):
        go_out[:, b] = jnp.transpose(rate[b]).reshape(GROUPS, 8, 128)
    pl.semaphore_wait(barrier, GROUPS - 1 + mp)

    def send(source, target, dst, out_sem, in_sem):
        pltpu.make_async_remote_copy(
            src_ref=source,
            dst_ref=target.at[me],
            send_sem=out_sem,
            recv_sem=in_sem,
            device_id={"stream": dst},
            device_id_type=MESH,
        ).start()

    first = [at(dy, dx) for dy, dx in FIRST]
    others = [at(dy, dx) for dy, dx in OTHERS]
    peers = first[:-1] + others
    for peer in peers:
        send(meta.at[me], meta, peer, meta_send, meta_recv)
    for peer in peers:
        send(go_out.at[peer], go_in, peer, go_send, go_recv.at[me])
    go_in[me] = go_out[me]

    sp_copy.wait()
    z_halo = [
        pltpu.make_async_remote_copy(
            sp.at[:, 7], zh.at[0], halo_send.at[0], halo_recv.at[0], device_id={"stream": after}, device_id_type=MESH
        ),
        pltpu.make_async_remote_copy(
            sp.at[:, 0], zh.at[1], halo_send.at[1], halo_recv.at[1], device_id={"stream": before}, device_id_type=MESH
        ),
    ]
    for copy in z_halo:
        copy.start()
    lane = iota((8, 16, 128), 2)
    packed = jnp.zeros((8, 16, 128), F32)
    for s in range(NS):
        turned = pltpu.roll(sp[s], 2 * s + 2, 2)
        packed = jnp.where((lane == 2 * s + 1) | (lane == 2 * s + 2), turned, packed)
    pack[...] = packed

    def send_share(dst):
        pltpu.make_async_remote_copy(
            share.at[mp], share.at[mp], share_send.at[dst], share_recv.at[mp], device_id={"span": dst}, device_id_type=MESH
        ).start()

    def wait_share(sem, k):
        pltpu.make_async_copy(share.at[k], share.at[k], sem.at[k]).wait()

    def halo_copy(slot, dst):
        return pltpu.make_async_remote_copy(
            pack, yh.at[slot], halo_send.at[2 + slot], halo_recv.at[2 + slot], device_id={"span": dst}, device_id_type=MESH
        )

    def wait_halo(sem, slot):
        pltpu.make_async_copy(yh.at[slot], yh.at[slot], sem.at[2 + slot]).wait()

    @pl.when(mp > 0)
    def _():
        halo_copy(1, mp - 1).start()

    for d in range(1, spans):

        @pl.when(mp >= d)
        def _():
            send_share(mp - d)

    some = meta.at[pl.ds(0, GROUPS - 1)]
    pltpu.make_async_copy(some, some, meta_recv).wait()
    cells = jnp.concatenate([meta[4 * q] + meta[4 * q + 1] + meta[4 * q + 2] + meta[4 * q + 3] for q in range(4)], axis=1)
    from_z = jnp.floor(cells * (1.0 / 16.0))
    from_x = cells - 16.0 * from_z
    row = iota((128, 512), 0)
    row_z = (row // 16).astype(F32) * (1.0 / 16.0)
    same_x = (row % 16).astype(F32) == from_x
    from_z = from_z * (1.0 / 16.0)

    def weights(dst):
        offset = row_z - (from_z - 0.5 * dst.astype(F32))
        weight = jnp.where(same_x, jnp.exp(-0.5 * offset * offset), 0.0)
        high = weight.astype(BF16)
        low = (weight - high.astype(F32)).astype(BF16)
        return jnp.concatenate([high, high, low], axis=1)

    for n, dst in enumerate(first):
        wts[n] = weights(dst)

    for peer in peers:
        pltpu.make_async_copy(go_in.at[peer], go_in.at[peer], go_recv.at[peer]).wait()
    quarter = iota((8, 128), 1) // 32

    def gathered(s, q):
        block, k = s // 4, s % 4
        value = go_in[4 * q, block]
        for i in range(1, 4):
            value = jnp.where(quarter == (k + i) % 4, go_in[4 * q + i, block], value)
        return value if k == 0 else pltpu.roll(value, 128 - 32 * k, 1)

    values = [jnp.concatenate([gathered(s, q) for q in range(4)], axis=1) for s in range(NS)]
    power = values[0] * values[0]
    for s in range(1, NS):
        power = power + values[s] * values[s]
    power = power * (1.0 / NS)
    values = jnp.concatenate(values + [power / (power + 1.0)], axis=0)
    high = values.astype(BF16)
    low = (values - high.astype(F32)).astype(BF16)
    left[...] = jnp.concatenate([high, low, high], axis=1)

    def product(right):
        return lax.dot_general(left[...], right, (((1,), (1,)), ((), ())), preferred_element_type=F32)

    def give(piece, dst):
        back_out[dst] = piece
        send(back_out.at[dst], back_in, dst, back_send, back_recv.at[me])

    for n in range(0, 8, 2):
        part = product(wts[n : n + 2].reshape(256, 1536))
        give(part[:, :128], first[n])
        if n + 1 < 7:
            give(part[:, 128:], first[n + 1])
        else:
            back_in[me] = part[:, 128:]

    steps_y = sum(dy << (2 * k) for k, (dy, _) in enumerate(OTHERS))
    steps_x = sum(dx << (2 * k) for k, (_, dx) in enumerate(OTHERS))

    def two_others(n, _):
        pair = []
        for k in range(2):
            shift = 4 * n + 2 * k
            dy = lax.shift_right_logical(jnp.int32(steps_y), shift) & 3
            dx = lax.shift_right_logical(jnp.int32(steps_x), shift) & 3
            pair.append(at(dy, dx))
        part = product(jnp.concatenate([weights(dst) for dst in pair], axis=0))
        for k, dst in enumerate(pair):
            give(part[:, 128 * k : 128 * k + 128], dst)
        return 0

    lax.fori_loop(0, 4, two_others, 0)

    @pl.when(mp < spans - 1)
    def _():
        wait_halo(halo_recv, 1)
        halo_copy(0, mp + 1).start()

    for d in range(1, spans):

        @pl.when(mp + d < spans)
        def _():
            wait_share(share_recv, mp + d)
            send_share(mp + d)

    for copy in z_halo:
        copy.wait()

    @pl.when(mp > 0)
    def _():
        wait_halo(halo_recv, 0)
        wait_halo(halo_send, 1)

    @pl.when(mp < spans - 1)
    def _():
        wait_halo(halo_send, 0)

    @pl.when(mp == 0)
    def _():
        yh[0] = jnp.zeros((8, 16, 128), F32)

    @pl.when(mp == spans - 1)
    def _():
        yh[1] = jnp.zeros((8, 16, 128), F32)

    below, above = me > 0, me < GROUPS - 1
    xs = iota((8, 16, 128), 1)
    edge = jnp.where(lane % 2 == 0, pltpu.roll(yh[1], 126, 2), yh[0])
    for s in range(NS):
        cells = sp[s]
        ends = pltpu.roll(edge, 127 - 2 * s, 2)
        zdown = jnp.concatenate([jnp.where(below, zh[0, s], 0.0)[None], cells[:-1]], axis=0)
        zup = jnp.concatenate([cells[1:], jnp.where(above, zh[1, s], 0.0)[None]], axis=0)
        xdown = jnp.where(xs == 0, 0.0, pltpu.roll(cells, 1, 1))
        xup = jnp.where(xs == 15, 0.0, pltpu.roll(cells, 15, 1))
        ydown = jnp.where(lane == 0, ends, pltpu.roll(cells, 1, 2))
        yup = jnp.where(lane == 127, ends, pltpu.roll(cells, 127, 2))
        spread[s] = zup + zdown + xup + xdown + yup + ydown - 6.0 * cells

    for d in range(1, spans):

        @pl.when(mp >= d)
        def _():
            wait_share(share_recv, mp - d)
            wait_share(share_send, mp - d)

        @pl.when(mp + d < spans)
        def _():
            wait_share(share_send, mp + d)

    lane2 = iota((1, 128), 1)
    owed = share[0]
    for g in range(1, spans):
        owed = owed + share[g]
    here = jnp.where(lane2 == mp, owed, 0.0)
    out[8 * NS] = jnp.broadcast_to(jnp.sum(here, axis=1, keepdims=True), (16, 128))

    peaks = []
    for z in range(8):
        wide = jnp.broadcast_to(levels[z], (16, 16))
        eye = iota((16, 16), 0) == iota((16, 16), 1)
        kind = jnp.sum(jnp.where(eye, wide.astype(F32), 0.0), axis=1, keepdims=True)
        peaks.append(jnp.where(kind == 0, 1.5, jnp.where(kind == 1, 4.0, jnp.where(kind == 2, 9.0, 19.0))))
    peak = jnp.concatenate(peaks, axis=0).astype(F32)

    cell_z = (iota((128, 128), 0) // 16 + 8 * me).astype(F32)
    offset = (cell_z - iota((128, 128), 1).astype(F32)) * (1.0 / 16.0)
    norm = 1.0 / jnp.sum(jnp.exp(-0.5 * offset * offset), axis=1, keepdims=True)
    peak = peak * norm
    norm = 4.0 * norm

    for peer in peers:
        pltpu.make_async_copy(back_in.at[peer], back_in.at[peer], back_recv.at[peer]).wait()

    def smoothed(s):
        return jnp.transpose(back_in[:, 8 * s : 8 * s + 8, :].reshape(128, 128))

    thick = 1.0 + peak * smoothed(NS)
    stretch = 0.02 * thick
    damp = norm / thick
    for s in range(NS):
        value = sp[s].reshape(128, 128) + stretch * spread[s].reshape(128, 128) + smoothed(s) * damp
        out[8 * s : 8 * s + 8] = value.reshape(8, 16, 128)
    for buffer, sem in ((meta, meta_send), (go_out, go_send), (back_out, back_send)):
        sent = buffer.at[pl.ds(0, GROUPS - 1)]
        pltpu.make_async_copy(sent, sent, sem).wait()


def deliver(both, out_hbm, load_hbm, load, sems):
    cells = both.at[pl.ds(0, 8 * NS)]
    copies = [
        pltpu.make_async_copy(cells, out_hbm, sems.at[0]),
        pltpu.make_async_copy(load, load_hbm, sems.at[1]),
    ]
    copies[0].start()
    load[...] = both[8 * NS, 0:1, 0:1].astype(jnp.int32)
    copies[1].start()
    for copy in copies:
        copy.wait()


def shards(spans, species, history, flame_tiles, owners, orders, substeps, levels, mechanism):
    states = jnp.transpose(history, (0, 1, 3, 4, 2, 5)).reshape(3, NS, 32, 128)
    vmem = pl.BlockSpec(memory_space=pltpu.VMEM)
    anywhere = pl.BlockSpec(memory_space=pl.ANY)
    both = pl.pallas_call(
        functools.partial(kernel, spans),
        out_shape=pltpu.VMEM((8 * NS + 1, 16, 128), F32),
        in_specs=[anywhere] * 8,
        out_specs=vmem,
        scratch_shapes=[
            pltpu.SMEM((NS, NS), F32),
            pltpu.VMEM((1, 32), jnp.int32),
            pltpu.VMEM((1, 32), jnp.int32),
            pltpu.VMEM((1, 32), jnp.int32),
            pltpu.VMEM((1, 32), jnp.int32),
            pltpu.VMEM((8, 1, 16), jnp.int32),
            pltpu.VMEM((3, NS, 32, 128), F32),
            pltpu.VMEM((NS, 8, 16, 128), F32),
            pltpu.VMEM((3, 128, 128), F32),
            pltpu.VMEM((GROUPS, 1, 128), F32),
            pltpu.VMEM((8, 128, 1536), BF16),
            pltpu.VMEM((80, 1536), BF16),
            pltpu.VMEM((GROUPS, 3, 8, 128), F32),
            pltpu.VMEM((GROUPS, 3, 8, 128), F32),
            pltpu.VMEM((GROUPS, 80, 128), F32),
            pltpu.VMEM((GROUPS, 80, 128), F32),
            pltpu.VMEM((spans, 1, 128), F32),
            pltpu.VMEM((9, 32, 128), F32),
            pltpu.VMEM((2, NS, 16, 128), F32),
            pltpu.VMEM((2, 8, 16, 128), F32),
            pltpu.VMEM((8, 16, 128), F32),
            pltpu.VMEM((NS, 8, 16, 128), F32),
            pltpu.SemaphoreType.DMA((6,)),
            pltpu.SemaphoreType.DMA,
            pltpu.SemaphoreType.DMA,
            pltpu.SemaphoreType.DMA,
            pltpu.SemaphoreType.DMA,
            pltpu.SemaphoreType.DMA,
            pltpu.SemaphoreType.DMA((GROUPS,)),
            pltpu.SemaphoreType.DMA,
            pltpu.SemaphoreType.DMA((GROUPS,)),
            pltpu.SemaphoreType.DMA((spans,)),
            pltpu.SemaphoreType.DMA((spans,)),
            pltpu.SemaphoreType.DMA((4,)),
            pltpu.SemaphoreType.DMA((4,)),
        ],
        compiler_params=pltpu.CompilerParams(
            collective_id=0, has_side_effects=True
        ),
    )(
        mechanism,
        species,
        states,
        flame_tiles.reshape(1, 32),
        owners.reshape(1, 32),
        orders.reshape(1, 32),
        substeps.reshape(1, 32),
        jnp.transpose(levels, (0, 2, 1)),
    )
    out, load = pl.pallas_call(
        deliver,
        out_shape=(
            jax.ShapeDtypeStruct((8 * NS, 16, 128), F32),
            jax.ShapeDtypeStruct((1, 1), jnp.int32),
        ),
        in_specs=[vmem],
        out_specs=(anywhere, anywhere),
        scratch_shapes=[pltpu.VMEM((1, 1), jnp.int32), pltpu.SemaphoreType.DMA((2,))],
        compiler_params=pltpu.CompilerParams(vmem_limit_bytes=2**20),
    )(both)
    return out.reshape(species.shape), load


def solution(mesh):
    in_specs = (
        P(None, "stream", None, "span"),
        P("stream", "span", None, None, None, None),
        P("stream", "span", None),
        P("stream", "span", None, None),
        P("stream", "span", None),
        P("stream", "span", None),
        P("stream", None, "span"),
        P(),
    )
    out_specs = (P(None, "stream", None, "span"), P("stream", "span"))
    return jax.shard_map(
        functools.partial(shards, mesh.shape["span"]),
        mesh=mesh,
        in_specs=in_specs,
        out_specs=out_specs,
        check_vma=False,
    )
```

```python
import functools

import jax
import jax.numpy as jnp
from jax import lax
from jax.experimental import pallas as pl
from jax.experimental.pallas import tpu as pltpu
from jax.sharding import PartitionSpec as P

MESH = pl.DeviceIdType.MESH
F32 = jnp.float32
BF16 = jnp.bfloat16
SUBMAX = 8
NS = 9
SIDE = 4
GROUPS = SIDE * SIDE
CHUNKS = 4
FIRST = ((1, 1), (3, 3), (2, 0), (3, 1), (1, 3), (2, 2), (2, 1), (0, 0))
OTHERS = ((2, 3), (1, 2), (3, 2), (1, 0), (3, 0), (0, 2), (0, 3), (0, 1))


def iota(shape, dim):
    return lax.broadcasted_iota(jnp.int32, shape, dim)


def by_order(order, one, two, three):
    return jnp.where(order == 1, F32(one), jnp.where(order == 2, F32(two), F32(three)))


def column(row, size):
    wide = jnp.broadcast_to(row.astype(F32), (size, size))
    eye = iota((size, size), 0) == iota((size, size), 1)
    return jnp.sum(jnp.where(eye, wide, 0.0), axis=1, keepdims=True)


def kernel(
    spans,
    mech_hbm,
    species_hbm,
    history_hbm,
    tiles_hbm,
    owners_hbm,
    orders_hbm,
    steps_hbm,
    levels_hbm,
    out,
    mech,
    tiles,
    owners,
    orders,
    steps,
    levels,
    hist,
    sp,
    rate,
    meta,
    wts,
    left,
    go_out,
    go_in,
    back_out,
    back_in,
    share,
    coef,
    zh,
    yh,
    pack,
    spread,
    table_sem,
    hist_sem,
    sp_sem,
    meta_send,
    meta_recv,
    go_send,
    go_recv,
    back_send,
    back_recv,
    share_send,
    share_recv,
    halo_send,
    halo_recv,
):
    me = lax.axis_index("stream")
    mp = lax.axis_index("span")
    sy, sx = me // SIDE, me % SIDE

    table_copies = [
        pltpu.make_async_copy(source, target, table_sem.at[k])
        for k, (source, target) in enumerate(
            (
                (orders_hbm, orders),
                (steps_hbm, steps),
                (tiles_hbm, tiles),
                (owners_hbm, owners),
                (mech_hbm, mech),
                (levels_hbm, levels),
            )
        )
    ]
    for copy in table_copies:
        copy.start()
    hist_copy = pltpu.make_async_copy(history_hbm, hist, hist_sem)
    hist_copy.start()
    sp_copy = pltpu.make_async_copy(species_hbm, sp, sp_sem)
    sp_copy.start()

    def at(dy, dx):
        return ((sy + dy + SIDE) % SIDE) * SIDE + (sx + dx + SIDE) % SIDE

    after, before = (me + 1) % GROUPS, (me + GROUPS - 1) % GROUPS
    barrier = pltpu.get_barrier_semaphore()
    for d in range(1, GROUPS):
        pl.semaphore_signal(barrier, inc=1, device_id={"stream": (me + d) % GROUPS}, device_id_type=MESH)
    for d in range(1, spans):

        @pl.when(mp + d < spans)
        def _():
            pl.semaphore_signal(barrier, inc=1, device_id={"span": mp + d}, device_id_type=MESH)

    for copy in table_copies:
        copy.wait()
    order = jnp.broadcast_to(column(orders[...], 32), (32, 128))
    count = column(steps[...], 32)
    tile = column(tiles[...], 32)
    owner = column(owners[...], 32)
    coef[0] = by_order(order, 1.0, 2.0, 3.0)
    coef[1] = by_order(order, 0.0, -1.0, -3.0)
    coef[2] = by_order(order, 0.0, 0.0, 1.0)
    coef[3] = by_order(order, 1.0, 4.0 / 3.0, 18.0 / 11.0)
    coef[4] = by_order(order, 0.0, -1.0 / 3.0, -9.0 / 11.0)
    coef[5] = by_order(order, 0.0, 0.0, 2.0 / 11.0)
    coef[6] = by_order(order, 0.5, 0.5 * 2.0 / 3.0, 0.5 * 6.0 / 11.0)
    count_b = jnp.broadcast_to(count, (32, 128))
    coef[7] = count_b
    coef[8] = 1.0 / jnp.maximum(count_b, 1.0)

    def place(s, c):
        return s // 4, pl.ds(pl.multiple_of(32 * ((s + me) % 4) + 8 * c, 8), 8)

    cell_of = jnp.broadcast_to(tile + (128 * me).astype(F32), (32, 128))
    mine = iota((32, 128), 1) == iota((32, 128), 0) + 32 * (me % 4)
    meta[me] = jnp.sum(jnp.where(mine, cell_of, 0.0), axis=0, keepdims=True)
    for c in range(CHUNKS):
        for s in (9, 10, 11):
            block, rows = place(s, c)
            rate[block, rows, :] = jnp.zeros((8, 128), F32)
    lane32 = iota((32, 128), 1).astype(F32)
    share[mp] = jnp.sum(jnp.where(owner == lane32, count_b, 0.0), axis=0, keepdims=True)

    def chemistry(c):
        rows = slice(8 * c, 8 * c + 8)
        p1, p2, p3, a1, a2, a3, hb, cnt, inv = [coef[k, rows, :] for k in range(9)]
        h1, h2, h3 = [tuple(hist[m, s, rows, :] for s in range(NS)) for m in range(3)]

        last = h1
        for n in range(SUBMAX):
            guess = [p1 * h1[s] + p2 * h2[s] + p3 * h3[s] for s in range(NS)]
            active = cnt > F32(n)
            fresh = []
            done = []
            for s in range(NS):
                total = mech[s, 0] * guess[0]
                for t in range(1, NS):
                    total = total + mech[s, t] * guess[t]
                y = a1 * h1[s] + a2 * h2[s] + a3 * h3[s] + hb * jnp.tanh(total)
                fresh.append(y)
                done.append(jnp.where(active, y, last[s]))
            h1, h2, h3, last = fresh, h1, h2, done
        for s in range(NS):
            block, spot = place(s, c)
            rate[block, spot, :] = (last[s] - hist[0, s, rows, :]) * inv

    hist_copy.wait()
    for c in range(CHUNKS):
        chemistry(c)
    for b in range(3):
        go_out[:, b] = jnp.transpose(rate[b]).reshape(GROUPS, 8, 128)
    pl.semaphore_wait(barrier, GROUPS - 1 + mp)

    def send(source, target, dst, out_sem, in_sem):
        pltpu.make_async_remote_copy(
            src_ref=source,
            dst_ref=target.at[me],
            send_sem=out_sem,
            recv_sem=in_sem,
            device_id={"stream": dst},
            device_id_type=MESH,
        ).start()

    first = [at(dy, dx) for dy, dx in FIRST]
    others = [at(dy, dx) for dy, dx in OTHERS]
    peers = first[:-1] + others
    for peer in peers:
        send(meta.at[me], meta, peer, meta_send, meta_recv)
    for peer in peers:
        send(go_out.at[peer], go_in, peer, go_send, go_recv.at[me])
    go_in[me] = go_out[me]

    sp_copy.wait()
    z_halo = [
        pltpu.make_async_remote_copy(
            sp.at[:, 7], zh.at[0], halo_send.at[0], halo_recv.at[0], device_id={"stream": after}, device_id_type=MESH
        ),
        pltpu.make_async_remote_copy(
            sp.at[:, 0], zh.at[1], halo_send.at[1], halo_recv.at[1], device_id={"stream": before}, device_id_type=MESH
        ),
    ]
    for copy in z_halo:
        copy.start()
    lane = iota((8, 16, 128), 2)
    packed = jnp.zeros((8, 16, 128), F32)
    for s in range(NS):
        turned = pltpu.roll(sp[s], 2 * s + 2, 2)
        packed = jnp.where((lane == 2 * s + 1) | (lane == 2 * s + 2), turned, packed)
    pack[...] = packed

    def send_share(dst):
        pltpu.make_async_remote_copy(
            share.at[mp], share.at[mp], share_send.at[dst], share_recv.at[mp], device_id={"span": dst}, device_id_type=MESH
        ).start()

    def wait_share(sem, k):
        pltpu.make_async_copy(share.at[k], share.at[k], sem.at[k]).wait()

    def halo_copy(slot, dst):
        return pltpu.make_async_remote_copy(
            pack, yh.at[slot], halo_send.at[2 + slot], halo_recv.at[2 + slot], device_id={"span": dst}, device_id_type=MESH
        )

    def wait_halo(sem, slot):
        pltpu.make_async_copy(yh.at[slot], yh.at[slot], sem.at[2 + slot]).wait()

    @pl.when(mp > 0)
    def _():
        halo_copy(1, mp - 1).start()

    for d in range(1, spans):

        @pl.when(mp >= d)
        def _():
            send_share(mp - d)

    some = meta.at[pl.ds(0, GROUPS - 1)]
    pltpu.make_async_copy(some, some, meta_recv).wait()
    cells = jnp.concatenate([meta[4 * q] + meta[4 * q + 1] + meta[4 * q + 2] + meta[4 * q + 3] for q in range(4)], axis=1)
    from_z = jnp.floor(cells * (1.0 / 16.0))
    from_x = cells - 16.0 * from_z
    row = iota((128, 512), 0)
    row_z = (row // 16).astype(F32) * (1.0 / 16.0)
    same_x = (row % 16).astype(F32) == from_x
    from_z = from_z * (1.0 / 16.0)

    def weights(dst):
        offset = row_z - (from_z - 0.5 * dst.astype(F32))
        weight = jnp.where(same_x, jnp.exp(-0.5 * offset * offset), 0.0)
        high = weight.astype(BF16)
        low = (weight - high.astype(F32)).astype(BF16)
        return jnp.concatenate([high, high, low], axis=1)

    for n, dst in enumerate(first):
        wts[n] = weights(dst)

    for peer in peers:
        pltpu.make_async_copy(go_in.at[peer], go_in.at[peer], go_recv.at[peer]).wait()
    quarter = iota((8, 128), 1) // 32

    def gathered(s, q):
        block, k = s // 4, s % 4
        value = go_in[4 * q, block]
        for i in range(1, 4):
            value = jnp.where(quarter == (k + i) % 4, go_in[4 * q + i, block], value)
        return value if k == 0 else pltpu.roll(value, 128 - 32 * k, 1)

    values = [jnp.concatenate([gathered(s, q) for q in range(4)], axis=1) for s in range(NS)]
    power = values[0] * values[0]
    for s in range(1, NS):
        power = power + values[s] * values[s]
    power = power * (1.0 / NS)
    values = jnp.concatenate(values + [power / (power + 1.0)], axis=0)
    high = values.astype(BF16)
    low = (values - high.astype(F32)).astype(BF16)
    left[...] = jnp.concatenate([high, low, high], axis=1)

    def product(right):
        return lax.dot_general(left[...], right, (((1,), (1,)), ((), ())), preferred_element_type=F32)

    def give(piece, dst):
        back_out[dst] = piece
        send(back_out.at[dst], back_in, dst, back_send, back_recv.at[me])

    for n in range(0, 8, 2):
        part = product(wts[n : n + 2].reshape(256, 1536))
        give(part[:, :128], first[n])
        if n + 1 < 7:
            give(part[:, 128:], first[n + 1])
        else:
            back_in[me] = part[:, 128:]

    steps_y = sum(dy << (2 * k) for k, (dy, _) in enumerate(OTHERS))
    steps_x = sum(dx << (2 * k) for k, (_, dx) in enumerate(OTHERS))

    def two_others(n, _):
        pair = []
        for k in range(2):
            shift = 4 * n + 2 * k
            dy = lax.shift_right_logical(jnp.int32(steps_y), shift) & 3
            dx = lax.shift_right_logical(jnp.int32(steps_x), shift) & 3
            pair.append(at(dy, dx))
        part = product(jnp.concatenate([weights(dst) for dst in pair], axis=0))
        for k, dst in enumerate(pair):
            give(part[:, 128 * k : 128 * k + 128], dst)
        return 0

    lax.fori_loop(0, 4, two_others, 0)

    @pl.when(mp < spans - 1)
    def _():
        wait_halo(halo_recv, 1)
        halo_copy(0, mp + 1).start()

    for d in range(1, spans):

        @pl.when(mp + d < spans)
        def _():
            wait_share(share_recv, mp + d)
            send_share(mp + d)

    for copy in z_halo:
        copy.wait()

    @pl.when(mp > 0)
    def _():
        wait_halo(halo_recv, 0)
        wait_halo(halo_send, 1)

    @pl.when(mp < spans - 1)
    def _():
        wait_halo(halo_send, 0)

    @pl.when(mp == 0)
    def _():
        yh[0] = jnp.zeros((8, 16, 128), F32)

    @pl.when(mp == spans - 1)
    def _():
        yh[1] = jnp.zeros((8, 16, 128), F32)

    below, above = me > 0, me < GROUPS - 1
    xs = iota((8, 16, 128), 1)
    edge = jnp.where(lane % 2 == 0, pltpu.roll(yh[1], 126, 2), yh[0])
    for s in range(NS):
        cells = sp[s]
        ends = pltpu.roll(edge, 127 - 2 * s, 2)
        zdown = jnp.concatenate([jnp.where(below, zh[0, s], 0.0)[None], cells[:-1]], axis=0)
        zup = jnp.concatenate([cells[1:], jnp.where(above, zh[1, s], 0.0)[None]], axis=0)
        xdown = jnp.where(xs == 0, 0.0, pltpu.roll(cells, 1, 1))
        xup = jnp.where(xs == 15, 0.0, pltpu.roll(cells, 15, 1))
        ydown = jnp.where(lane == 0, ends, pltpu.roll(cells, 1, 2))
        yup = jnp.where(lane == 127, ends, pltpu.roll(cells, 127, 2))
        spread[s] = zup + zdown + xup + xdown + yup + ydown - 6.0 * cells

    for d in range(1, spans):

        @pl.when(mp >= d)
        def _():
            wait_share(share_recv, mp - d)
            wait_share(share_send, mp - d)

        @pl.when(mp + d < spans)
        def _():
            wait_share(share_send, mp + d)

    lane2 = iota((1, 128), 1)
    owed = share[0]
    for g in range(1, spans):
        owed = owed + share[g]
    here = jnp.where(lane2 == mp, owed, 0.0)
    out[8 * NS] = jnp.broadcast_to(jnp.sum(here, axis=1, keepdims=True), (16, 128))

    peaks = []
    for z in range(8):
        wide = jnp.broadcast_to(levels[z], (16, 16))
        eye = iota((16, 16), 0) == iota((16, 16), 1)
        kind = jnp.sum(jnp.where(eye, wide.astype(F32), 0.0), axis=1, keepdims=True)
        peaks.append(jnp.where(kind == 0, 1.5, jnp.where(kind == 1, 4.0, jnp.where(kind == 2, 9.0, 19.0))))
    peak = jnp.concatenate(peaks, axis=0).astype(F32)

    cell_z = (iota((128, 128), 0) // 16 + 8 * me).astype(F32)
    offset = (cell_z - iota((128, 128), 1).astype(F32)) * (1.0 / 16.0)
    norm = 1.0 / jnp.sum(jnp.exp(-0.5 * offset * offset), axis=1, keepdims=True)
    peak = peak * norm
    norm = 4.0 * norm

    for peer in peers:
        pltpu.make_async_copy(back_in.at[peer], back_in.at[peer], back_recv.at[peer]).wait()

    def smoothed(s):
        return jnp.transpose(back_in[:, 8 * s : 8 * s + 8, :].reshape(128, 128))

    thick = 1.0 + peak * smoothed(NS)
    stretch = 0.02 * thick
    damp = norm / thick
    for s in range(NS):
        value = sp[s].reshape(128, 128) + stretch * spread[s].reshape(128, 128) + smoothed(s) * damp
        out[8 * s : 8 * s + 8] = value.reshape(8, 16, 128)
    for buffer, sem in ((meta, meta_send), (go_out, go_send), (back_out, back_send)):
        sent = buffer.at[pl.ds(0, GROUPS - 1)]
        pltpu.make_async_copy(sent, sent, sem).wait()


def deliver(both, out_hbm, load_hbm, load, sems):
    cells = both.at[pl.ds(0, 8 * NS)]
    copies = [
        pltpu.make_async_copy(cells, out_hbm, sems.at[0]),
        pltpu.make_async_copy(load, load_hbm, sems.at[1]),
    ]
    copies[0].start()
    load[...] = both[8 * NS, 0:1, 0:1].astype(jnp.int32)
    copies[1].start()
    for copy in copies:
        copy.wait()


def shards(spans, species, history, flame_tiles, owners, orders, substeps, levels, mechanism):
    states = jnp.transpose(history, (0, 1, 3, 4, 2, 5)).reshape(3, NS, 32, 128)
    vmem = pl.BlockSpec(memory_space=pltpu.VMEM)
    anywhere = pl.BlockSpec(memory_space=pl.ANY)
    both = pl.pallas_call(
        functools.partial(kernel, spans),
        out_shape=pltpu.VMEM((8 * NS + 1, 16, 128), F32),
        in_specs=[anywhere] * 8,
        out_specs=vmem,
        scratch_shapes=[
            pltpu.SMEM((NS, NS), F32),
            pltpu.VMEM((1, 32), jnp.int32),
            pltpu.VMEM((1, 32), jnp.int32),
            pltpu.VMEM((1, 32), jnp.int32),
            pltpu.VMEM((1, 32), jnp.int32),
            pltpu.VMEM((8, 1, 16), jnp.int32),
            pltpu.VMEM((3, NS, 32, 128), F32),
            pltpu.VMEM((NS, 8, 16, 128), F32),
            pltpu.VMEM((3, 128, 128), F32),
            pltpu.VMEM((GROUPS, 1, 128), F32),
            pltpu.VMEM((8, 128, 1536), BF16),
            pltpu.VMEM((80, 1536), BF16),
            pltpu.VMEM((GROUPS, 3, 8, 128), F32),
            pltpu.VMEM((GROUPS, 3, 8, 128), F32),
            pltpu.VMEM((GROUPS, 80, 128), F32),
            pltpu.VMEM((GROUPS, 80, 128), F32),
            pltpu.VMEM((spans, 1, 128), F32),
            pltpu.VMEM((9, 32, 128), F32),
            pltpu.VMEM((2, NS, 16, 128), F32),
            pltpu.VMEM((2, 8, 16, 128), F32),
            pltpu.VMEM((8, 16, 128), F32),
            pltpu.VMEM((NS, 8, 16, 128), F32),
            pltpu.SemaphoreType.DMA((6,)),
            pltpu.SemaphoreType.DMA,
            pltpu.SemaphoreType.DMA,
            pltpu.SemaphoreType.DMA,
            pltpu.SemaphoreType.DMA,
            pltpu.SemaphoreType.DMA,
            pltpu.SemaphoreType.DMA((GROUPS,)),
            pltpu.SemaphoreType.DMA,
            pltpu.SemaphoreType.DMA((GROUPS,)),
            pltpu.SemaphoreType.DMA((spans,)),
            pltpu.SemaphoreType.DMA((spans,)),
            pltpu.SemaphoreType.DMA((4,)),
            pltpu.SemaphoreType.DMA((4,)),
        ],
        compiler_params=pltpu.CompilerParams(
            collective_id=0, has_side_effects=True
        ),
    )(
        mechanism,
        species,
        states,
        flame_tiles.reshape(1, 32),
        owners.reshape(1, 32),
        orders.reshape(1, 32),
        substeps.reshape(1, 32),
        jnp.transpose(levels, (0, 2, 1)),
    )
    out, load = pl.pallas_call(
        deliver,
        out_shape=(
            jax.ShapeDtypeStruct((8 * NS, 16, 128), F32),
            jax.ShapeDtypeStruct((1, 1), jnp.int32),
        ),
        in_specs=[vmem],
        out_specs=(anywhere, anywhere),
        scratch_shapes=[pltpu.VMEM((1, 1), jnp.int32), pltpu.SemaphoreType.DMA((2,))],
        compiler_params=pltpu.CompilerParams(vmem_limit_bytes=2**20),
    )(both)
    return out.reshape(species.shape), load


def solution(mesh):
    in_specs = (
        P(None, "stream", None, "span"),
        P("stream", "span", None, None, None, None),
        P("stream", "span", None),
        P("stream", "span", None, None),
        P("stream", "span", None),
        P("stream", "span", None),
        P("stream", None, "span"),
        P(),
    )
    out_specs = (P(None, "stream", None, "span"), P("stream", "span"))
    return jax.shard_map(
        functools.partial(shards, mesh.shape["span"]),
        mesh=mesh,
        in_specs=in_specs,
        out_specs=out_specs,
        check_vma=False,
    )
```

```python
import functools

import jax
import jax.numpy as jnp
from jax import lax
from jax.experimental import pallas as pl
from jax.experimental.pallas import tpu as pltpu
from jax.sharding import PartitionSpec as P

MESH = pl.DeviceIdType.MESH
F32 = jnp.float32
BF16 = jnp.bfloat16
SUBMAX = 8
NS = 9
SIDE = 4
GROUPS = SIDE * SIDE
CHUNKS = 4
FIRST = ((1, 1), (3, 3), (2, 0), (3, 1), (1, 3), (2, 2), (2, 1), (0, 0))
OTHERS = ((2, 3), (1, 2), (3, 2), (1, 0), (3, 0), (0, 2), (0, 3), (0, 1))


def iota(shape, dim):
    return lax.broadcasted_iota(jnp.int32, shape, dim)


def by_order(order, one, two, three):
    return jnp.where(order == 1, F32(one), jnp.where(order == 2, F32(two), F32(three)))


def column(row, size):
    wide = jnp.broadcast_to(row.astype(F32), (size, size))
    eye = iota((size, size), 0) == iota((size, size), 1)
    return jnp.sum(jnp.where(eye, wide, 0.0), axis=1, keepdims=True)


def kernel(
    spans,
    mech_hbm,
    species_hbm,
    history_hbm,
    tiles_hbm,
    owners_hbm,
    orders_hbm,
    steps_hbm,
    levels_hbm,
    out,
    mech,
    tiles,
    owners,
    orders,
    steps,
    levels,
    hist,
    sp,
    rate,
    meta,
    wts,
    left,
    go_out,
    go_in,
    back_out,
    back_in,
    share,
    coef,
    zh,
    yh,
    pack,
    spread,
    table_sem,
    hist_sem,
    sp_sem,
    meta_send,
    meta_recv,
    go_send,
    go_recv,
    back_send,
    back_recv,
    share_send,
    share_recv,
    halo_send,
    halo_recv,
):
    me = lax.axis_index("stream")
    mp = lax.axis_index("span")
    sy, sx = me // SIDE, me % SIDE

    table_copies = [
        pltpu.make_async_copy(source, target, table_sem.at[k])
        for k, (source, target) in enumerate(
            (
                (orders_hbm, orders),
                (steps_hbm, steps),
                (tiles_hbm, tiles),
                (owners_hbm, owners),
                (mech_hbm, mech),
                (levels_hbm, levels),
            )
        )
    ]
    for copy in table_copies:
        copy.start()
    hist_copy = pltpu.make_async_copy(history_hbm, hist, hist_sem)
    hist_copy.start()
    sp_copy = pltpu.make_async_copy(species_hbm, sp, sp_sem)
    sp_copy.start()

    def at(dy, dx):
        return ((sy + dy + SIDE) % SIDE) * SIDE + (sx + dx + SIDE) % SIDE

    after, before = (me + 1) % GROUPS, (me + GROUPS - 1) % GROUPS
    barrier = pltpu.get_barrier_semaphore()
    for dy, dx in sorted(FIRST[:-1] + OTHERS, key=lambda step: -(min(step[0], 4 - step[0]) + min(step[1], 4 - step[1]))):
        pl.semaphore_signal(barrier, inc=1, device_id={"stream": at(dy, dx)}, device_id_type=MESH)
    for d in range(1, spans):

        @pl.when(mp + d < spans)
        def _():
            pl.semaphore_signal(barrier, inc=1, device_id={"span": mp + d}, device_id_type=MESH)

    for copy in table_copies:
        copy.wait()
    order = jnp.broadcast_to(column(orders[...], 32), (32, 128))
    count = column(steps[...], 32)
    tile = column(tiles[...], 32)
    owner = column(owners[...], 32)
    coef[0] = by_order(order, 1.0, 2.0, 3.0)
    coef[1] = by_order(order, 0.0, -1.0, -3.0)
    coef[2] = by_order(order, 0.0, 0.0, 1.0)
    coef[3] = by_order(order, 1.0, 4.0 / 3.0, 18.0 / 11.0)
    coef[4] = by_order(order, 0.0, -1.0 / 3.0, -9.0 / 11.0)
    coef[5] = by_order(order, 0.0, 0.0, 2.0 / 11.0)
    coef[6] = by_order(order, 0.5, 0.5 * 2.0 / 3.0, 0.5 * 6.0 / 11.0)
    count_b = jnp.broadcast_to(count, (32, 128))
    coef[7] = count_b
    coef[8] = 1.0 / jnp.maximum(count_b, 1.0)

    def place(s, c):
        return s // 4, pl.ds(pl.multiple_of(32 * ((s + me) % 4) + 8 * c, 8), 8)

    cell_of = jnp.broadcast_to(tile + (128 * me).astype(F32), (32, 128))
    mine = iota((32, 128), 1) == iota((32, 128), 0) + 32 * (me % 4)
    meta[me] = jnp.sum(jnp.where(mine, cell_of, 0.0), axis=0, keepdims=True)
    for c in range(CHUNKS):
        for s in (9, 10, 11):
            block, rows = place(s, c)
            rate[block, rows, :] = jnp.zeros((8, 128), F32)
    lane32 = iota((32, 128), 1).astype(F32)
    share[mp] = jnp.sum(jnp.where(owner == lane32, count_b, 0.0), axis=0, keepdims=True)

    def chemistry(c):
        rows = slice(8 * c, 8 * c + 8)
        p1, p2, p3, a1, a2, a3, hb, cnt, inv = [coef[k, rows, :] for k in range(9)]
        h1, h2, h3 = [tuple(hist[m, s, rows, :] for s in range(NS)) for m in range(3)]

        last = h1
        for n in range(SUBMAX):
            guess = [p1 * h1[s] + p2 * h2[s] + p3 * h3[s] for s in range(NS)]
            active = cnt > F32(n)
            fresh = []
            done = []
            for s in range(NS):
                total = mech[s, 0] * guess[0]
                for t in range(1, NS):
                    total = total + mech[s, t] * guess[t]
                y = a1 * h1[s] + a2 * h2[s] + a3 * h3[s] + hb * jnp.tanh(total)
                fresh.append(y)
                done.append(jnp.where(active, y, last[s]))
            h1, h2, h3, last = fresh, h1, h2, done
        for s in range(NS):
            block, spot = place(s, c)
            rate[block, spot, :] = (last[s] - hist[0, s, rows, :]) * inv

    hist_copy.wait()
    for c in range(CHUNKS):
        chemistry(c)
    for b in range(3):
        go_out[:, b] = jnp.transpose(rate[b]).reshape(GROUPS, 8, 128)
    pl.semaphore_wait(barrier, GROUPS - 1 + mp)

    def send(source, target, dst, out_sem, in_sem):
        pltpu.make_async_remote_copy(
            src_ref=source,
            dst_ref=target.at[me],
            send_sem=out_sem,
            recv_sem=in_sem,
            device_id={"stream": dst},
            device_id_type=MESH,
        ).start()

    first = [at(dy, dx) for dy, dx in FIRST]
    others = [at(dy, dx) for dy, dx in OTHERS]
    peers = first[:-1] + others
    for peer in peers:
        send(meta.at[me], meta, peer, meta_send, meta_recv)
    for peer in peers:
        send(go_out.at[peer], go_in, peer, go_send, go_recv.at[me])
    go_in[me] = go_out[me]

    sp_copy.wait()
    z_halo = [
        pltpu.make_async_remote_copy(
            sp.at[:, 7], zh.at[0], halo_send.at[0], halo_recv.at[0], device_id={"stream": after}, device_id_type=MESH
        ),
        pltpu.make_async_remote_copy(
            sp.at[:, 0], zh.at[1], halo_send.at[1], halo_recv.at[1], device_id={"stream": before}, device_id_type=MESH
        ),
    ]
    for copy in z_halo:
        copy.start()
    lane = iota((8, 16, 128), 2)
    packed = jnp.zeros((8, 16, 128), F32)
    for s in range(NS):
        turned = pltpu.roll(sp[s], 2 * s + 2, 2)
        packed = jnp.where((lane == 2 * s + 1) | (lane == 2 * s + 2), turned, packed)
    pack[...] = packed

    def send_share(dst):
        pltpu.make_async_remote_copy(
            share.at[mp], share.at[mp], share_send.at[dst], share_recv.at[mp], device_id={"span": dst}, device_id_type=MESH
        ).start()

    def wait_share(sem, k):
        pltpu.make_async_copy(share.at[k], share.at[k], sem.at[k]).wait()

    def halo_copy(slot, dst):
        return pltpu.make_async_remote_copy(
            pack, yh.at[slot], halo_send.at[2 + slot], halo_recv.at[2 + slot], device_id={"span": dst}, device_id_type=MESH
        )

    def wait_halo(sem, slot):
        pltpu.make_async_copy(yh.at[slot], yh.at[slot], sem.at[2 + slot]).wait()

    @pl.when(mp > 0)
    def _():
        halo_copy(1, mp - 1).start()

    for d in range(1, spans):

        @pl.when(mp >= d)
        def _():
            send_share(mp - d)

    some = meta.at[pl.ds(0, GROUPS - 1)]
    pltpu.make_async_copy(some, some, meta_recv).wait()
    cells = jnp.concatenate([meta[4 * q] + meta[4 * q + 1] + meta[4 * q + 2] + meta[4 * q + 3] for q in range(4)], axis=1)
    from_z = jnp.floor(cells * (1.0 / 16.0))
    from_x = cells - 16.0 * from_z
    row = iota((128, 512), 0)
    row_z = (row // 16).astype(F32) * (1.0 / 16.0)
    same_x = (row % 16).astype(F32) == from_x
    from_z = from_z * (1.0 / 16.0)

    def weights(dst):
        offset = row_z - (from_z - 0.5 * dst.astype(F32))
        weight = jnp.where(same_x, jnp.exp(-0.5 * offset * offset), 0.0)
        high = weight.astype(BF16)
        low = (weight - high.astype(F32)).astype(BF16)
        return jnp.concatenate([high, high, low], axis=1)

    for n, dst in enumerate(first):
        wts[n] = weights(dst)

    for peer in peers:
        pltpu.make_async_copy(go_in.at[peer], go_in.at[peer], go_recv.at[peer]).wait()
    quarter = iota((8, 128), 1) // 32

    def gathered(s, q):
        block, k = s // 4, s % 4
        value = go_in[4 * q, block]
        for i in range(1, 4):
            value = jnp.where(quarter == (k + i) % 4, go_in[4 * q + i, block], value)
        return value if k == 0 else pltpu.roll(value, 128 - 32 * k, 1)

    values = [jnp.concatenate([gathered(s, q) for q in range(4)], axis=1) for s in range(NS)]
    power = values[0] * values[0]
    for s in range(1, NS):
        power = power + values[s] * values[s]
    power = power * (1.0 / NS)
    values = jnp.concatenate(values + [power / (power + 1.0)], axis=0)
    high = values.astype(BF16)
    low = (values - high.astype(F32)).astype(BF16)
    left[...] = jnp.concatenate([high, low, high], axis=1)

    def product(right):
        return lax.dot_general(left[...], right, (((1,), (1,)), ((), ())), preferred_element_type=F32)

    def give(piece, dst):
        back_out[dst] = piece
        send(back_out.at[dst], back_in, dst, back_send, back_recv.at[me])

    for n in range(0, 8, 2):
        part = product(wts[n : n + 2].reshape(256, 1536))
        give(part[:, :128], first[n])
        if n + 1 < 7:
            give(part[:, 128:], first[n + 1])
        else:
            back_in[me] = part[:, 128:]

    steps_y = sum(dy << (2 * k) for k, (dy, _) in enumerate(OTHERS))
    steps_x = sum(dx << (2 * k) for k, (_, dx) in enumerate(OTHERS))

    def two_others(n, _):
        pair = []
        for k in range(2):
            shift = 4 * n + 2 * k
            dy = lax.shift_right_logical(jnp.int32(steps_y), shift) & 3
            dx = lax.shift_right_logical(jnp.int32(steps_x), shift) & 3
            pair.append(at(dy, dx))
        part = product(jnp.concatenate([weights(dst) for dst in pair], axis=0))
        for k, dst in enumerate(pair):
            give(part[:, 128 * k : 128 * k + 128], dst)
        return 0

    lax.fori_loop(0, 4, two_others, 0)

    @pl.when(mp < spans - 1)
    def _():
        wait_halo(halo_recv, 1)
        halo_copy(0, mp + 1).start()

    for d in range(1, spans):

        @pl.when(mp + d < spans)
        def _():
            wait_share(share_recv, mp + d)
            send_share(mp + d)

    for copy in z_halo:
        copy.wait()

    @pl.when(mp > 0)
    def _():
        wait_halo(halo_recv, 0)
        wait_halo(halo_send, 1)

    @pl.when(mp < spans - 1)
    def _():
        wait_halo(halo_send, 0)

    @pl.when(mp == 0)
    def _():
        yh[0] = jnp.zeros((8, 16, 128), F32)

    @pl.when(mp == spans - 1)
    def _():
        yh[1] = jnp.zeros((8, 16, 128), F32)

    below, above = me > 0, me < GROUPS - 1
    xs = iota((8, 16, 128), 1)
    edge = jnp.where(lane % 2 == 0, pltpu.roll(yh[1], 126, 2), yh[0])
    for s in range(NS):
        cells = sp[s]
        ends = pltpu.roll(edge, 127 - 2 * s, 2)
        zdown = jnp.concatenate([jnp.where(below, zh[0, s], 0.0)[None], cells[:-1]], axis=0)
        zup = jnp.concatenate([cells[1:], jnp.where(above, zh[1, s], 0.0)[None]], axis=0)
        xdown = jnp.where(xs == 0, 0.0, pltpu.roll(cells, 1, 1))
        xup = jnp.where(xs == 15, 0.0, pltpu.roll(cells, 15, 1))
        ydown = jnp.where(lane == 0, ends, pltpu.roll(cells, 1, 2))
        yup = jnp.where(lane == 127, ends, pltpu.roll(cells, 127, 2))
        spread[s] = zup + zdown + xup + xdown + yup + ydown - 6.0 * cells

    for d in range(1, spans):

        @pl.when(mp >= d)
        def _():
            wait_share(share_recv, mp - d)
            wait_share(share_send, mp - d)

        @pl.when(mp + d < spans)
        def _():
            wait_share(share_send, mp + d)

    lane2 = iota((1, 128), 1)
    owed = share[0]
    for g in range(1, spans):
        owed = owed + share[g]
    here = jnp.where(lane2 == mp, owed, 0.0)
    out[8 * NS] = jnp.broadcast_to(jnp.sum(here, axis=1, keepdims=True), (16, 128))

    peaks = []
    for z in range(8):
        wide = jnp.broadcast_to(levels[z], (16, 16))
        eye = iota((16, 16), 0) == iota((16, 16), 1)
        kind = jnp.sum(jnp.where(eye, wide.astype(F32), 0.0), axis=1, keepdims=True)
        peaks.append(jnp.where(kind == 0, 1.5, jnp.where(kind == 1, 4.0, jnp.where(kind == 2, 9.0, 19.0))))
    peak = jnp.concatenate(peaks, axis=0).astype(F32)

    cell_z = (iota((128, 128), 0) // 16 + 8 * me).astype(F32)
    offset = (cell_z - iota((128, 128), 1).astype(F32)) * (1.0 / 16.0)
    norm = 1.0 / jnp.sum(jnp.exp(-0.5 * offset * offset), axis=1, keepdims=True)
    peak = peak * norm
    norm = 4.0 * norm

    for peer in peers:
        pltpu.make_async_copy(back_in.at[peer], back_in.at[peer], back_recv.at[peer]).wait()

    def smoothed(s):
        return jnp.transpose(back_in[:, 8 * s : 8 * s + 8, :].reshape(128, 128))

    thick = 1.0 + peak * smoothed(NS)
    stretch = 0.02 * thick
    damp = norm / thick
    for s in range(NS):
        value = sp[s].reshape(128, 128) + stretch * spread[s].reshape(128, 128) + smoothed(s) * damp
        out[8 * s : 8 * s + 8] = value.reshape(8, 16, 128)
    for buffer, sem in ((meta, meta_send), (go_out, go_send), (back_out, back_send)):
        sent = buffer.at[pl.ds(0, GROUPS - 1)]
        pltpu.make_async_copy(sent, sent, sem).wait()


def deliver(both, out_hbm, load_hbm, load, sems):
    cells = both.at[pl.ds(0, 8 * NS)]
    copies = [
        pltpu.make_async_copy(cells, out_hbm, sems.at[0]),
        pltpu.make_async_copy(load, load_hbm, sems.at[1]),
    ]
    copies[0].start()
    load[...] = both[8 * NS, 0:1, 0:1].astype(jnp.int32)
    copies[1].start()
    for copy in copies:
        copy.wait()


def shards(spans, species, history, flame_tiles, owners, orders, substeps, levels, mechanism):
    states = jnp.transpose(history, (0, 1, 3, 4, 2, 5)).reshape(3, NS, 32, 128)
    vmem = pl.BlockSpec(memory_space=pltpu.VMEM)
    anywhere = pl.BlockSpec(memory_space=pl.ANY)
    both = pl.pallas_call(
        functools.partial(kernel, spans),
        out_shape=pltpu.VMEM((8 * NS + 1, 16, 128), F32),
        in_specs=[anywhere] * 8,
        out_specs=vmem,
        scratch_shapes=[
            pltpu.SMEM((NS, NS), F32),
            pltpu.VMEM((1, 32), jnp.int32),
            pltpu.VMEM((1, 32), jnp.int32),
            pltpu.VMEM((1, 32), jnp.int32),
            pltpu.VMEM((1, 32), jnp.int32),
            pltpu.VMEM((8, 1, 16), jnp.int32),
            pltpu.VMEM((3, NS, 32, 128), F32),
            pltpu.VMEM((NS, 8, 16, 128), F32),
            pltpu.VMEM((3, 128, 128), F32),
            pltpu.VMEM((GROUPS, 1, 128), F32),
            pltpu.VMEM((8, 128, 1536), BF16),
            pltpu.VMEM((80, 1536), BF16),
            pltpu.VMEM((GROUPS, 3, 8, 128), F32),
            pltpu.VMEM((GROUPS, 3, 8, 128), F32),
            pltpu.VMEM((GROUPS, 80, 128), F32),
            pltpu.VMEM((GROUPS, 80, 128), F32),
            pltpu.VMEM((spans, 1, 128), F32),
            pltpu.VMEM((9, 32, 128), F32),
            pltpu.VMEM((2, NS, 16, 128), F32),
            pltpu.VMEM((2, 8, 16, 128), F32),
            pltpu.VMEM((8, 16, 128), F32),
            pltpu.VMEM((NS, 8, 16, 128), F32),
            pltpu.SemaphoreType.DMA((6,)),
            pltpu.SemaphoreType.DMA,
            pltpu.SemaphoreType.DMA,
            pltpu.SemaphoreType.DMA,
            pltpu.SemaphoreType.DMA,
            pltpu.SemaphoreType.DMA,
            pltpu.SemaphoreType.DMA((GROUPS,)),
            pltpu.SemaphoreType.DMA,
            pltpu.SemaphoreType.DMA((GROUPS,)),
            pltpu.SemaphoreType.DMA((spans,)),
            pltpu.SemaphoreType.DMA((spans,)),
            pltpu.SemaphoreType.DMA((4,)),
            pltpu.SemaphoreType.DMA((4,)),
        ],
        compiler_params=pltpu.CompilerParams(
            collective_id=0, has_side_effects=True
        ),
    )(
        mechanism,
        species,
        states,
        flame_tiles.reshape(1, 32),
        owners.reshape(1, 32),
        orders.reshape(1, 32),
        substeps.reshape(1, 32),
        jnp.transpose(levels, (0, 2, 1)),
    )
    out, load = pl.pallas_call(
        deliver,
        out_shape=(
            jax.ShapeDtypeStruct((8 * NS, 16, 128), F32),
            jax.ShapeDtypeStruct((1, 1), jnp.int32),
        ),
        in_specs=[vmem],
        out_specs=(anywhere, anywhere),
        scratch_shapes=[pltpu.VMEM((1, 1), jnp.int32), pltpu.SemaphoreType.DMA((2,))],
        compiler_params=pltpu.CompilerParams(vmem_limit_bytes=2**20),
    )(both)
    return out.reshape(species.shape), load


def solution(mesh):
    in_specs = (
        P(None, "stream", None, "span"),
        P("stream", "span", None, None, None, None),
        P("stream", "span", None),
        P("stream", "span", None, None),
        P("stream", "span", None),
        P("stream", "span", None),
        P("stream", None, "span"),
        P(),
    )
    out_specs = (P(None, "stream", None, "span"), P("stream", "span"))
    return jax.shard_map(
        functools.partial(shards, mesh.shape["span"]),
        mesh=mesh,
        in_specs=in_specs,
        out_specs=out_specs,
        check_vma=False,
    )
```
